32 devices in a mesh: net: 8 (over z, x), mem: 4 (over y, core).
Axes of the slice: x: 2, y: 2, z: 4, core: 2. Of those that a mesh axis runs over, the one named last changes fastest.
Arguments:
- stored_reach_flows: bfloat16 [5, 128, 32768], P(None, 'mem', 'net'), may hold values from 0.19921875 to 5
- lateral: bfloat16 [4, 128, 32768], P(None, 'mem', 'net'), may hold values from 0.049804688 to 1
- cotangent: bfloat16 [4, 128, 32768], P(None, 'mem', 'net'), may hold values from -3 to 3
- roughness: float32 [32768], P('net'), may hold values from 0.02 to 0.1
- travel_factor: float32 [32768], P('net'), may hold values from 0.2 to 5
- inverse_block_matrix: float32 [256, 128, 128], P('net'), may hold values from 0 to 1, as said below
- down_in_block: int32 [32768], P('net'), may hold values from 1 to 128, as said below
- exit_slot: int32 [32768], P('net'), may hold values from -1 to 127, as said below
- inlet_reach: int32 [8, 128], P('net'), may hold values from 1 to 3999, as said below
Outputs:
- grad_lateral: bfloat16 [4, 128, 32768], P(None, 'mem', 'net')
- grad_rough: float32 [32768], P(('net', 'mem'))
The draws below stay inside these ranges and needn't reach their ends.
Inputs may be any that keep to these rules, and one draw needn't show every extreme that they name: Within a block a reach feeds a later position: down_in_block[r] > r % 128 where it is under 128. exit_slot[r] >= 0 only where down_in_block[r] == 128 and r is not in the last partition; every reach of the last partition has -1. `inlet_reach`: each entry is a reach at positions 1 to 31 of some block of that partition; several slots may name the same reach. inverse_block_matrix[k][i, j] is 1 where i = j, the product of weight_new over the reaches after j up to and including i where i lies on the in-block path of next reaches from j, and 0 elsewhere.
All inputs are finite; a program needn't handle non-finite values.
Results may differ from the reference program's by a relative error of at most 0.001.
Values sent between devices are 32-bit elements; how exact they have to be, the bound alone decides.
No kernel may reach another device: no remote copies, remote signals or barrier semaphores. Data moves between devices by JAX's collectives and lax.ppermute only.
A program may use at most 64 MiB of HBM per device.

```python
import math
import jax
import jax.numpy as jnp
from jax import lax

NBLK = 32
NIN = 128
STEPS = 4
R_DEV = 4096
REACHES = 32768
MEMBERS = 128
N_NET = 8


def link_layout(key):
    link_key = jax.random.fold_in(key, 11)
    slot_key = jax.random.fold_in(key, 12)
    head_key = jax.random.fold_in(key, 13)
    partitions = REACHES // R_DEV
    slot_ids = jnp.arange(NIN, dtype=jnp.int32)[None, :]
    head_pos = jax.random.randint(head_key, (partitions, NIN), 1, 32, dtype=jnp.int32)
    head_pos = jnp.where(slot_ids == NIN - 1, 31, jnp.where(slot_ids == 0, 1, head_pos))
    inlets = (slot_ids % NBLK * 128 + head_pos).astype(jnp.int32)
    reach_ids = jnp.arange(REACHES, dtype=jnp.int32)
    position = reach_ids % 128
    stride = jax.random.randint(jax.random.fold_in(link_key, 1), (REACHES,), 1, 9, dtype=jnp.int32)
    retained_values = jax.random.randint(jax.random.fold_in(link_key, 2), (REACHES,), 0, 100, dtype=jnp.int32)
    target = position + stride
    down_pos = jnp.where((retained_values < 85) & (target <= 127), target, 128)
    inlet_global = (jnp.arange(partitions, dtype=jnp.int32)[:, None] * R_DEV + inlets).reshape(-1)
    marked = jnp.zeros((REACHES,), dtype=bool).at[inlet_global].set(True)
    down_pos = jnp.where(marked, 128, down_pos)
    down_pos = jnp.where(reach_ids == 0, 1, down_pos).astype(jnp.int32)
    partition = reach_ids // R_DEV
    slot_pick = jax.random.randint(slot_key, (REACHES,), 0, NIN, dtype=jnp.int32)
    slot_pick = jnp.where(reach_ids % R_DEV == 127, NIN - 1, slot_pick)
    boundary = (down_pos == 128) & (partition < partitions - 1)
    exit_ids = jnp.where(boundary, slot_pick, -1).astype(jnp.int32)
    return (down_pos, exit_ids, inlets, marked)


def coefficient_draws(key):
    rough_key = jax.random.fold_in(key, 21)
    factor_key = jax.random.fold_in(key, 22)
    marked = link_layout(key)[3]
    roughness_uniform = jax.random.uniform(rough_key, (REACHES,), jnp.float32)
    travel_factor_uniform = jax.random.uniform(factor_key, (REACHES,), jnp.float32)
    roughness_draw = jnp.exp(jnp.log(0.02) + roughness_uniform * (jnp.log(0.1) - jnp.log(0.02)))
    fast_factor = jnp.exp(jnp.log(0.2) + travel_factor_uniform * (jnp.log(0.5) - jnp.log(0.2)))
    slow_factor = jnp.exp(jnp.log(0.5) + travel_factor_uniform * (jnp.log(5.0) - jnp.log(0.5)))
    roughness_draw = jnp.clip(roughness_draw, 0.02, 0.1).astype(jnp.float32)
    factor_draw = jnp.clip(jnp.where(marked, fast_factor, slow_factor), 0.2, 5.0).astype(jnp.float32)
    return (roughness_draw, factor_draw)


def draw_roughness(key, part):
    return coefficient_draws(key)[0]


def draw_travel_factor(key, part):
    return coefficient_draws(key)[1]


def draw_down_in_block(key, part):
    return link_layout(key)[0]


def draw_exit_slot(key, part):
    return link_layout(key)[1]


def draw_inlet_reach(key, part):
    return link_layout(key)[2]


def draw_inverse_block_matrix(key, part):
    down_pos = link_layout(key)[0]
    roughness_draw, factor_draw = coefficient_draws(key)
    travel = roughness_draw * factor_draw
    divisor = 0.8 * travel + 0.5
    weight_new = (0.5 - 0.2 * travel) / divisor
    block_count = REACHES // 128
    down_blocks = down_pos.reshape(block_count, 128)
    weight_blocks = weight_new.reshape(block_count, 128)
    row_ids = jnp.arange(128, dtype=jnp.int32)

    def column_step(counter, matrix):
        position = 127 - counter
        target = lax.dynamic_index_in_dim(down_blocks, position, 1, False)
        interior_reaches = target < 128
        clipped = jnp.minimum(target, 127).astype(jnp.int32)
        path_gain = jnp.take_along_axis(weight_blocks, clipped[:, None], axis=1)[:, 0]
        path_gain = jnp.where(interior_reaches, path_gain, 0.0)
        index_grid = jnp.broadcast_to(clipped[:, None, None], (block_count, 128, 1))
        downstream = jnp.take_along_axis(matrix, index_grid, axis=2)
        unit_column = jnp.where(row_ids == position, 1.0, 0.0).astype(jnp.float32)[None, :, None]
        column_new = unit_column + path_gain[:, None, None] * downstream
        return lax.dynamic_update_slice_in_dim(matrix, column_new.astype(jnp.float32), position, axis=2)
    start_matrix = jnp.zeros((block_count, 128, 128), jnp.float32)
    return lax.fori_loop(0, 128, column_step, start_matrix).astype(jnp.float32)


def block_scale(rng, shape, pieces, least, high):
    loudness = 1.0
    for dim, blocks in pieces:
        heights = jax.random.uniform(jax.random.fold_in(jax.random.fold_in(rng, 6), dim), (blocks,), jnp.float32, least / len(pieces), high / len(pieces))
        loudness = loudness * jnp.repeat(jnp.exp(heights), shape[dim] // blocks).reshape((-1,) + (1,) * (len(shape) - 1 - dim))
    return loudness


def gaussian(stream_key, extent, spread, most, shards=(), kind=jnp.bfloat16):
    array = jax.random.normal(stream_key, extent, jnp.float32) * spread
    if len(shards) > 0:
        array = block_scale(stream_key, extent, shards, -0.22, 0.18) * array
    return jnp.clip(array, min=-most, max=most).astype(kind)


def setup_inputs(seed: int = 0) -> dict:
    key_list = jax.random.split(jax.random.key(seed), 10)
    stored_reach_flows = jnp.clip(jnp.exp(math.log(5.0) - 3.2227897 * jax.random.uniform(key_list[0], (STEPS + 1, MEMBERS, REACHES), jnp.float32) ** block_scale(key_list[0], (STEPS + 1, MEMBERS, REACHES), ((1, 4), (2, 8)), -0.2, 0.2)), 0.19921875, 5.0).astype(jnp.bfloat16)
    lateral = jnp.clip(jnp.exp(math.log(1.0) - 2.9996462 * jax.random.uniform(key_list[1], (STEPS, MEMBERS, REACHES), jnp.float32) ** block_scale(key_list[1], (STEPS, MEMBERS, REACHES), ((1, 4), (2, 8)), -0.2, 0.2)), 0.049804688, 1.0).astype(jnp.bfloat16)
    cotangent = gaussian(key_list[2], (STEPS, MEMBERS, REACHES), 0.5, 3.0, ((1, 4), (2, 8)))
    roughness = draw_roughness(jax.random.fold_in(key_list[9], 71), 0)
    travel_factor = draw_travel_factor(jax.random.fold_in(key_list[9], 71), 0)
    inverse_block_matrix = draw_inverse_block_matrix(jax.random.fold_in(key_list[9], 71), 0)
    down_in_block = draw_down_in_block(jax.random.fold_in(key_list[9], 71), 0)
    exit_slot = draw_exit_slot(jax.random.fold_in(key_list[9], 71), 0)
    inlet_reach = draw_inlet_reach(jax.random.fold_in(key_list[9], 71), 0)
    return dict(stored_reach_flows=stored_reach_flows, lateral=lateral, cotangent=cotangent, roughness=roughness, travel_factor=travel_factor, inverse_block_matrix=inverse_block_matrix, down_in_block=down_in_block, exit_slot=exit_slot, inlet_reach=inlet_reach)


skew_weight = 0.2


def coefficients(roughness, travel_factor):
    travel = roughness * travel_factor
    divisor = travel * (1.0 - skew_weight) + 0.5
    weight_new = (0.5 - travel * skew_weight) / divisor
    weight_old = (0.5 + travel * skew_weight) / divisor
    weight_stay = (travel * (1.0 - skew_weight) - 0.5) / divisor
    weight_side = 1.0 / divisor
    square = divisor * divisor
    updated_slope = -0.5 / square
    slope_old = (skew_weight - 0.5) / square
    slope_stay = (1.0 - skew_weight) / square
    slope_side = (skew_weight - 1.0) / square
    return (weight_new, weight_old, weight_stay, weight_side), (updated_slope, slope_old, slope_stay, slope_side)


def reference(stored_reach_flows, lateral, cotangent, roughness, travel_factor, inverse_block_matrix, down_in_block, exit_slot, inlet_reach):
    weights, slopes = coefficients(roughness, travel_factor)
    weight_new, weight_old, weight_stay, weight_side = weights
    updated_slope, slope_old, slope_stay, slope_side = slopes
    reach_ids = jnp.arange(REACHES, dtype=jnp.int32)
    part_ids = reach_ids // R_DEV
    block_start = (reach_ids // 128) * 128
    next_part = jnp.minimum(part_ids + 1, N_NET - 1)
    inlet_global = next_part * R_DEV + inlet_reach[next_part, jnp.maximum(exit_slot, 0)]
    down_reach = jnp.where(down_in_block < 128, block_start + down_in_block,
                           jnp.where(exit_slot >= 0, inlet_global, REACHES)).astype(jnp.int32)
    crossing = exit_slot >= 0

    def inflow_of(current_instant):
        flow_level = stored_reach_flows[current_instant].astype(jnp.float32)
        summed = jax.ops.segment_sum(flow_level.T, down_reach, num_segments=REACHES + 1)
        return summed[:REACHES].T

    adjoint_next = jnp.zeros((MEMBERS, REACHES), jnp.float32)
    grad_total = jnp.zeros((REACHES,), jnp.float32)
    lateral_grads = [None] * STEPS
    for counter in range(STEPS):
        current_instant = STEPS - counter
        padded = jnp.concatenate([weight_old * adjoint_next, jnp.zeros((MEMBERS, 1), jnp.float32)], axis=1)
        pulled = jnp.take(padded, down_reach, axis=1)
        source = cotangent[current_instant - 1].astype(jnp.float32) + weight_stay * adjoint_next + pulled
        adjoint_parts = [None] * N_NET
        for partition in reversed(range(N_NET)):
            offset = partition * R_DEV
            right_side = source[:, offset:offset + R_DEV]
            if partition + 1 < N_NET:
                weighted_down = adjoint_parts[partition + 1] * weight_new[offset + R_DEV:offset + 2 * R_DEV]
                local_index = inlet_reach[partition + 1][jnp.maximum(exit_slot[offset:offset + R_DEV], 0)]
                external = jnp.where(crossing[offset:offset + R_DEV][None, :],
                                     jnp.take(weighted_down, local_index, axis=1), 0.0)
                right_side = right_side + external
            reshaped_values = right_side.reshape(MEMBERS, NBLK, 128)
            inverse_portion = inverse_block_matrix[partition * NBLK:(partition + 1) * NBLK]
            solved_adjoint = jnp.einsum("acj,cjv->acv", reshaped_values, inverse_portion, precision=lax.Precision.HIGHEST)
            adjoint_parts[partition] = solved_adjoint.reshape(MEMBERS, R_DEV)
        adjoint = jnp.concatenate(adjoint_parts, axis=1)
        factor = (updated_slope * inflow_of(current_instant) + slope_old * inflow_of(current_instant - 1)
                  + slope_stay * stored_reach_flows[current_instant - 1].astype(jnp.float32)
                  + slope_side * lateral[current_instant - 1].astype(jnp.float32))
        grad_total = grad_total + jnp.sum(adjoint * factor, axis=0)
        lateral_grads[current_instant - 1] = (weight_side * adjoint).astype(jnp.bfloat16)
        adjoint_next = adjoint
    return jnp.stack(lateral_grads), travel_factor * grad_total
```

```python
import functools

import jax
import jax.numpy as jnp
from jax import lax
from jax.experimental import pallas as pl
from jax.experimental.pallas import tpu as pltpu
from jax.sharding import PartitionSpec as P

skew_weight = 0.2
LANES = 128
EXTRA = 8
F32 = jnp.float32


def take(values, index):
    return jnp.take_along_axis(values, index, axis=1, mode="promise_in_bounds")


def weights_of(travel):
    divisor = travel * (1.0 - skew_weight) + 0.5
    weight_new = (0.5 - travel * skew_weight) / divisor
    weight_old = (0.5 + travel * skew_weight) / divisor
    weight_stay = (travel * (1.0 - skew_weight) - 0.5) / divisor
    return weight_new, weight_old, weight_stay


def slopes_of(travel):
    divisor = travel * (1.0 - skew_weight) + 0.5
    square = divisor * divisor
    return (
        -0.5 / square,
        (skew_weight - 0.5) / square,
        (1.0 - skew_weight) / square,
        (skew_weight - 1.0) / square,
    )


def levels_of(lanes):
    count = 0
    while (1 << count) < lanes:
        count += 1
    return count


def local_kernel(
    steps, members, blocks,
    cot_ref, rough_ref, factor_ref, down_ref, exit_ref, inlet_ref,
    own_ref, message_ref, response_ref, slot_ref, inlet_values_ref, inlet_rows_ref,
    pointer_ref, gain_ref, stay_ref, ratio_ref,
):
    levels = levels_of(LANES)
    travel = rough_ref[...] * factor_ref[...]
    weight_new, weight_old, weight_stay = weights_of(travel)
    down = down_ref[...]
    lane = lax.broadcasted_iota(jnp.int32, down.shape, 1)
    interior = down < LANES
    pointer = jnp.where(interior, down, lane)
    next_new = take(weight_new, pointer)
    next_old = take(weight_old, pointer)
    gain = jnp.where(interior, next_new, 0.0)
    ratio = jnp.where(interior, next_old / next_new, 0.0)
    stay_ref[...] = weight_stay
    ratio_ref[...] = ratio
    pointers, gains = [], []
    for level in range(levels):
        pointers.append(pointer)
        gains.append(gain)
        pointer_ref[level] = pointer
        gain_ref[level] = gain
        gain = gain * take(gain, pointer)
        pointer = take(pointer, pointer)
    slot = take(exit_ref[...], pointer)
    reached = slot >= 0
    slot = jnp.maximum(slot, 0)
    slot_ref[...] = slot
    right = jnp.where(exit_ref[...] >= 0, 1.0, 0.0).astype(F32)
    responses = []
    for lag in range(steps):
        value = right
        for level in range(levels):
            value = value + gains[level] * take(value, pointers[level])
        responses.append(value)
        response_ref[lag] = value
        right = weight_stay * value + ratio * (value - right)

    inlet = inlet_ref[...]
    inlet_block = inlet // LANES
    inlet_lane = inlet - inlet_block * LANES
    lane_rows = jnp.broadcast_to(inlet_lane, (blocks, LANES))
    block_rows = lax.broadcasted_iota(jnp.int32, (blocks, LANES), 0)
    chosen = block_rows == jnp.broadcast_to(inlet_block, (blocks, LANES))

    def at_inlets(rows):
        return jnp.sum(jnp.where(chosen, take(rows, lane_rows), 0.0), axis=0, keepdims=True)

    travel_in = at_inlets(travel)
    slot_in = at_inlets(jnp.where(reached, slot, 0).astype(F32))
    response_in = [at_inlets(value) for value in responses]
    new_in, old_in, _ = weights_of(travel_in)

    member_lane = jnp.broadcast_to(inlet_lane, (members, LANES))
    member_block = jnp.broadcast_to(inlet_block, (members, LANES))
    inlet_values_ref[...] = jnp.zeros_like(inlet_values_ref)

    def one_block(block, carry):
        place = pl.ds(pl.multiple_of(block * LANES, LANES), LANES)
        row = pl.ds(block, 1)
        shape = (members, LANES)
        stay = jnp.broadcast_to(stay_ref[row, :], shape)
        rate = jnp.broadcast_to(ratio_ref[row, :], shape)
        here = member_block == block
        right = None
        value = None
        for step in reversed(range(steps)):
            source = cot_ref[step, :, place].astype(F32)
            right = source if value is None else source + stay * value + rate * (value - right)
            value = right
            for level in range(levels):
                index = jnp.broadcast_to(pointer_ref[level, row, :], shape)
                gain = jnp.broadcast_to(gain_ref[level, row, :], shape)
                value = value + gain * take(value, index)
            own_ref[step, :, place] = value
            rows = pl.ds(step * members, members)
            inlet_values_ref[rows, :] = jnp.where(
                here, take(value, member_lane), inlet_values_ref[rows, :]
            )
        return carry

    lax.fori_loop(0, blocks, one_block, 0, unroll=2)

    for step in range(steps):
        rows = pl.ds(step * members, members)
        outgoing = new_in * inlet_values_ref[rows, :]
        if step + 1 < steps:
            outgoing = outgoing + old_in * inlet_values_ref[pl.ds((step + 1) * members, members), :]
        message_ref[rows, :] = outgoing
    tail = []
    for lag in range(steps):
        coefficient = new_in * response_in[lag]
        if lag > 0:
            coefficient = coefficient + old_in * response_in[lag - 1]
        tail.append(coefficient)
    tail.append(slot_in)
    while len(tail) < EXTRA:
        tail.append(jnp.zeros_like(slot_in))
    message_ref[pl.ds(steps * members, EXTRA), :] = jnp.concatenate(tail, axis=0)
    aside = list(response_in) + [travel_in, slot_in]
    while len(aside) < EXTRA:
        aside.append(jnp.zeros_like(slot_in))
    inlet_rows_ref[...] = jnp.concatenate(aside, axis=0)


def compose(steps, members, upper, lower):
    values, coefficients, slot = upper
    below, below_coefficients, below_slot = lower
    index = jnp.broadcast_to(slot, (members, LANES)).astype(jnp.int32)
    pulled = [take(value, index) for value in below]
    result = []
    for step in range(steps):
        total = values[step]
        for lag in range(steps - step):
            total = total + coefficients[lag] * pulled[step + lag]
        result.append(total)
    if below_coefficients is None:
        return result, None, None
    table = jnp.concatenate(list(below_coefficients) + [below_slot], axis=0)
    pad = (-table.shape[0]) % 8
    if pad:
        table = jnp.concatenate([table, jnp.zeros((pad, LANES), F32)], axis=0)
    table = take(table, jnp.broadcast_to(slot, table.shape).astype(jnp.int32))
    combined = []
    for lag in range(steps):
        total = coefficients[0] * table[lag:lag + 1]
        for first in range(1, lag + 1):
            total = total + coefficients[first] * table[lag - first:lag - first + 1]
        combined.append(total)
    return result, combined, table[steps:steps + 1]


def read_message(steps, members, ref):
    values = [ref[pl.ds(step * members, members), :] for step in range(steps)]
    tail = ref[pl.ds(steps * members, EXTRA), :]
    return values, [tail[lag:lag + 1] for lag in range(steps)], tail[steps:steps + 1]


def write_message(steps, members, ref, message):
    values, coefficients, slot = message
    for step in range(steps):
        ref[pl.ds(step * members, members), :] = values[step]
    rows = list(coefficients) + [slot]
    while len(rows) < EXTRA:
        rows.append(jnp.zeros_like(slot))
    ref[pl.ds(steps * members, EXTRA), :] = jnp.concatenate(rows, axis=0)


def identity_message(steps, members):
    zero = jnp.zeros((members, LANES), F32)
    row = jnp.zeros((1, LANES), F32)
    lane = lax.broadcasted_iota(jnp.int32, (8, LANES), 1).astype(F32)[0:1]
    return [zero] * steps, [row + 1.0] + [row] * (steps - 1), lane


def digit_of(axis, stride, radix):
    return (lax.axis_index(axis) // stride) % radix


def group_kernel(steps, members, axis, stride, radix, final, has_inner, *refs):
    messages = refs[:radix]
    rest = refs[radix:]
    inner = rest[0] if has_inner else None
    outs = rest[1:] if has_inner else rest
    digit = digit_of(axis, stride, radix)
    for mine in range(radix):
        @pl.when(digit == mine)
        def _(mine=mine):
            def message(other):
                return read_message(steps, members, messages[source_of(mine, other, radix)])

            if final:
                value = [jnp.zeros((members, LANES), F32)] * steps
                for other in reversed(range(mine + 1, radix)):
                    if other == radix - 1:
                        value = message(other)[0]
                    else:
                        value = compose(steps, members, message(other), (value, None, None))[0]
                if has_inner and mine < radix - 1:
                    within = read_message(steps, members, inner)
                    value = compose(steps, members, within, (value, None, None))[0]
                elif has_inner:
                    value = read_message(steps, members, inner)[0]
                for step in range(steps):
                    outs[0][pl.ds(step * members, members), :] = value[step]
                return
            total = None
            later = None
            for other in reversed(range(radix)):
                total = message(other) if total is None else compose(steps, members, message(other), total)
                if other == mine + 1:
                    later = total
            if later is None:
                later = identity_message(steps, members)
            if has_inner:
                later = compose(steps, members, read_message(steps, members, inner), later)
            write_message(steps, members, outs[0], later)
            write_message(steps, members, outs[1], total)


def is_power(number):
    return number & (number - 1) == 0


def source_of(mine, other, radix):
    return mine ^ other if is_power(radix) else (other - mine) % radix


def exchange(value, axis, stride, radix, offset):
    pairs = []
    for device in range(lax.axis_size(axis)):
        digit = (device // stride) % radix
        source = digit ^ offset if is_power(radix) else (digit + offset) % radix
        pairs.append((device + (source - digit) * stride, device))
    return lax.ppermute(value, axis, pairs)


def radices_of(count):
    radices = []
    while count > 1:
        radix = next(r for r in (4, 2, 3, 5, 7, count) if count % r == 0)
        radices.append(radix)
        count //= radix
    return radices


def flow_kernel(
    steps, members, blocks,
    flow_ref, lateral_ref, rough_ref, factor_ref, down_ref, exit_ref,
    weight_ref, leaving_ref, slopes_ref,
):
    slopes = slopes_of(rough_ref[...] * factor_ref[...])
    for i in range(4):
        slopes_ref[i] = slopes[i]
    leaving_ref[...] = jnp.zeros_like(leaving_ref)
    sub = lax.broadcasted_iota(jnp.int32, (LANES, LANES), 0)

    def one_block(block, carry):
        place = pl.ds(pl.multiple_of(block * LANES, LANES), LANES)
        row = pl.ds(block, 1)
        into = (sub == jnp.broadcast_to(down_ref[row, :], (LANES, LANES)))
        leave = (sub == jnp.broadcast_to(exit_ref[row, :], (LANES, LANES)))
        table = jnp.concatenate([into, leave], axis=0).astype(F32).astype(jnp.bfloat16)
        flows = flow_ref[:, :, place].reshape((steps + 1) * members, LANES)
        summed = lax.dot_general(
            flows, table, (((1,), (1,)), ((), ())), preferred_element_type=F32
        )
        leaving_ref[...] += summed[:, LANES:]
        inflow = summed[:, :LANES]
        new, old, stay, side = (slopes_ref[i, row, :] for i in range(4))
        for step in range(steps):
            now = inflow[(step + 1) * members:(step + 2) * members]
            prior = inflow[step * members:(step + 1) * members]
            weight_ref[step, :, place] = (
                new * now
                + old * prior
                + stay * flow_ref[step, :, place].astype(F32)
                + side * lateral_ref[step, :, place].astype(F32)
            )
        return carry

    lax.fori_loop(0, blocks, one_block, 0, unroll=2)


def final_kernel(
    steps, members, blocks, ranks,
    incoming_ref, own_ref, response_ref, slot_ref, weight_ref, rough_ref, factor_ref,
    inlet_values_ref, inlet_rows_ref, arriving_ref, inlet_ref,
    grad_ref, *rest,
):
    pieces, (part_ref, side_ref) = rest[:ranks], rest[ranks:]
    travel = rough_ref[...] * factor_ref[...]
    side_ref[...] = 1.0 / (travel * (1.0 - skew_weight) + 0.5)
    shape = (members, LANES)

    def one_block(block, carry):
        place = pl.ds(pl.multiple_of(block * LANES, LANES), LANES)
        row = pl.ds(block, 1)
        index = jnp.broadcast_to(slot_ref[row, :], shape)
        response = [response_ref[lag, row, :] for lag in range(steps)]
        side = side_ref[row, :]
        pulled = [
            take(incoming_ref[pl.ds(step * members, members), :], index) for step in range(steps)
        ]
        total = jnp.zeros(shape, F32)
        for step in range(steps):
            value = own_ref[step, :, place]
            for lag in range(steps - step):
                value = value + response[lag] * pulled[step + lag]
            grad_ref[step, :, place] = (side * value).astype(jnp.bfloat16)
            total = total + value * weight_ref[step, :, place]
        part_ref[row, :] = jnp.sum(total, axis=0, keepdims=True)
        return carry

    lax.fori_loop(0, blocks, one_block, 0, unroll=2)

    rows = inlet_rows_ref[...]
    slope_new, slope_old, _, _ = slopes_of(rows[steps:steps + 1])
    index = jnp.broadcast_to(rows[steps + 1:steps + 2], shape).astype(jnp.int32)
    pulled = [
        take(incoming_ref[pl.ds(step * members, members), :], index) for step in range(steps)
    ]
    total = jnp.zeros(shape, F32)
    for step in range(steps):
        value = inlet_values_ref[pl.ds(step * members, members), :]
        for lag in range(steps - step):
            value = value + rows[lag:lag + 1] * pulled[step + lag]
        total = total + value * (
            slope_new * arriving_ref[pl.ds((step + 1) * members, members), :]
            + slope_old * arriving_ref[pl.ds(step * members, members), :]
        )
    at_inlet = jnp.sum(total, axis=0, keepdims=True)
    inlet = inlet_ref[...]
    inlet_block = inlet // LANES
    inlet_lane = inlet - inlet_block * LANES
    block_rows = lax.broadcasted_iota(jnp.int32, (blocks, LANES), 0)
    spread = jnp.where(block_rows == inlet_block, at_inlet, 0.0)
    lane_table = (
        lax.broadcasted_iota(jnp.int32, (LANES, LANES), 0)
        == jnp.broadcast_to(inlet_lane, (LANES, LANES))
    ).astype(F32)
    placed = lax.dot_general(
        spread, lane_table, (((1,), (1,)), ((), ())),
        precision=lax.Precision.HIGHEST, preferred_element_type=F32,
    )
    part_ref[...] = factor_ref[...] * (part_ref[...] + placed)
    mine = lax.axis_index("mem")
    piece = blocks // ranks
    for offset in range(ranks):
        target = mine ^ offset if is_power(ranks) else (mine + offset) % ranks
        pieces[offset][...] = part_ref[pl.ds(pl.multiple_of(target * piece, piece), piece), :]


def call(kernel, out_shape, scratch=(), flops=0, size=0, name=None):
    return pl.pallas_call(
        kernel,
        out_shape=out_shape,
        scratch_shapes=scratch,
        cost_estimate=pl.CostEstimate(flops=flops, bytes_accessed=size, transcendentals=0),
        name=name,
    )


def body(
    stored_reach_flows, lateral, cotangent, roughness, travel_factor,
    inverse_block_matrix, down_in_block, exit_slot, inlet_reach,
):
    steps, members, reaches = cotangent.shape
    blocks = reaches // LANES
    count = lax.axis_size("net")
    ranks = lax.axis_size("mem")
    rough = roughness.reshape(blocks, LANES)
    factor = travel_factor.reshape(blocks, LANES)
    down = down_in_block.reshape(blocks, LANES)
    leave = exit_slot.reshape(blocks, LANES)
    rows = steps * members + EXTRA
    shape = jax.ShapeDtypeStruct

    own, message, response, slot, inlet_values, inlet_rows = call(
        functools.partial(local_kernel, steps, members, blocks),
        (
            shape((steps, members, reaches), F32),
            shape((rows, LANES), F32),
            shape((steps, blocks, LANES), F32),
            shape((blocks, LANES), jnp.int32),
            shape((steps * members, LANES), F32),
            shape((EXTRA, LANES), F32),
        ),
        scratch=[
            pltpu.VMEM((levels_of(LANES), blocks, LANES), jnp.int32),
            pltpu.VMEM((levels_of(LANES), blocks, LANES), F32),
            pltpu.VMEM((blocks, LANES), F32),
            pltpu.VMEM((blocks, LANES), F32),
        ],
        flops=2 * 7 * steps * members * reaches,
        size=6 * steps * members * reaches,
        name="local",
    )(cotangent, rough, factor, down, leave, inlet_reach)

    weight, leaving = pl.pallas_call(
        functools.partial(flow_kernel, steps, members, blocks),
        out_shape=(
            shape((steps, members, reaches), F32),
            shape(((steps + 1) * members, LANES), F32),
        ),
        scratch_shapes=[pltpu.VMEM((4, blocks, LANES), F32)],
        cost_estimate=pl.CostEstimate(
            flops=4 * 128 * (steps + 1) * members * reaches,
            bytes_accessed=8 * steps * members * reaches, transcendentals=0,
        ),
        name="flows",
    )(stored_reach_flows, lateral, rough, factor, down, leave)
    arriving = lax.ppermute(leaving, "net", [(i, i + 1) for i in range(count - 1)])

    stride = 1
    inner = None
    radices = radices_of(count)
    incoming = None
    for turn, radix in enumerate(radices):
        final = turn == len(radices) - 1
        received = [message] + [
            exchange(message, "net", stride, radix, offset) for offset in range(1, radix)
        ]
        has_inner = inner is not None
        args = received + ([inner] if has_inner else [])
        out = shape((steps * members, LANES), F32) if final else (shape((rows, LANES), F32),) * 2
        result = call(
            functools.partial(group_kernel, steps, members, "net", stride, radix, final, has_inner),
            out, flops=20 * radix * rows * LANES, size=4 * radix * rows * LANES, name="compose",
        )(*args)
        if final:
            incoming = result
        else:
            inner, message = result
        stride *= radix
    if incoming is None:
        incoming = jnp.zeros((steps * members, LANES), F32)

    piece = shape((blocks // ranks, LANES), F32)
    grad_lateral, *pieces = call(
        functools.partial(final_kernel, steps, members, blocks, ranks),
        (shape((steps, members, reaches), jnp.bfloat16),) + (piece,) * ranks,
        scratch=[pltpu.VMEM((blocks, LANES), F32), pltpu.VMEM((blocks, LANES), F32)],
        flops=30 * steps * members * reaches,
        size=10 * steps * members * reaches,
        name="finish",
    )(
        incoming, own, response, slot, weight, rough, factor,
        inlet_values, inlet_rows, arriving, inlet_reach,
    )
    total = pieces[0]
    for offset in range(1, ranks):
        total = total + exchange(pieces[offset], "mem", 1, ranks, (ranks - offset) % ranks if not is_power(ranks) else offset)
    return grad_lateral, total.reshape(-1)


def solution(mesh):
    in_specs = (
        P(None, "mem", "net"),
        P(None, "mem", "net"),
        P(None, "mem", "net"),
        P("net"),
        P("net"),
        P("net", None, None),
        P("net"),
        P("net"),
        P("net", None),
    )
    out_specs = (P(None, "mem", "net"), P(("net", "mem")))
    return jax.shard_map(body, mesh=mesh, in_specs=in_specs, out_specs=out_specs, check_vma=False)
```

```python
import functools

import jax
import jax.numpy as jnp
from jax import lax
from jax.experimental import pallas as pl
from jax.experimental.pallas import tpu as pltpu
from jax.sharding import PartitionSpec as P

skew_weight = 0.2
LANES = 128
EXTRA = 8
F32 = jnp.float32


ROW_GATHER = lax.GatherDimensionNumbers(
    offset_dims=(), collapsed_slice_dims=(1,), start_index_map=(1,),
    operand_batching_dims=(0,), start_indices_batching_dims=(0,),
)
VMEM_BYTES = 20 << 20
GROUP = 8


def take(values, index):
    return lax.gather(
        values, index[..., None], ROW_GATHER, (1, 1),
        mode=lax.GatherScatterMode.PROMISE_IN_BOUNDS,
    )


def weights_of(travel):
    divisor = travel * (1.0 - skew_weight) + 0.5
    weight_new = (0.5 - travel * skew_weight) / divisor
    weight_old = (0.5 + travel * skew_weight) / divisor
    weight_stay = (travel * (1.0 - skew_weight) - 0.5) / divisor
    return weight_new, weight_old, weight_stay


def slopes_of(travel):
    divisor = travel * (1.0 - skew_weight) + 0.5
    square = divisor * divisor
    return (
        -0.5 / square,
        (skew_weight - 0.5) / square,
        (1.0 - skew_weight) / square,
        (skew_weight - 1.0) / square,
    )


def levels_of(lanes):
    count = 0
    while (1 << count) < lanes:
        count += 1
    return count


def split(value):
    high = value.astype(jnp.bfloat16)
    return high, (value - high.astype(F32)).astype(jnp.bfloat16)


def multiply_series(steps, left, right):
    result = []
    for lag in range(steps):
        total = left[0] * right[lag]
        for first in range(1, lag + 1):
            total = total + left[first] * right[lag - first]
        result.append(total)
    return result


def local_kernel(
    steps, members, blocks,
    cot_ref, matrix_ref, rough_ref, factor_ref, down_ref, exit_ref, inlet_ref,
    own_ref, message_ref, response_ref, slot_ref, inlet_values_ref, inlet_rows_ref,
    stay_ref, ratio_ref,
):
    travel = rough_ref[...] * factor_ref[...]
    weight_new, weight_old, weight_stay = weights_of(travel)
    down = down_ref[...]
    lane = lax.broadcasted_iota(jnp.int32, down.shape, 1)
    interior = down < LANES
    pointer = jnp.where(interior, down, lane)
    next_new = take(weight_new, pointer)
    next_old = take(weight_old, pointer)
    ratio = jnp.where(interior, next_old / next_new, 0.0)
    stay_ref[...] = weight_stay
    ratio_ref[...] = ratio

    inlet = inlet_ref[...]
    inlet_block = inlet // LANES
    inlet_lane = inlet - inlet_block * LANES
    member_lane = jnp.broadcast_to(inlet_lane, (members, LANES))
    member_block = jnp.broadcast_to(inlet_block, (members, LANES))
    at_inlet = [jnp.zeros((members, LANES), F32)] * steps

    def solve_group(first, at_inlet):
        places = range(first, min(first + GROUP, blocks))
        tables = {
            block: jnp.concatenate(split(matrix_ref[block]), axis=1) for block in places
        }
        right, value = {}, {}
        for step in reversed(range(steps)):
            for block in places:
                lanes = pl.ds(block * LANES, LANES)
                row = pl.ds(block, 1)
                source = cot_ref[step, :, lanes]
                if step == steps - 1:
                    right[block] = source.astype(F32)
                    product = jnp.dot(source, tables[block], preferred_element_type=F32)
                    value[block] = product[:, :LANES] + product[:, LANES:]
                else:
                    right[block] = (
                        source.astype(F32)
                        + stay_ref[row, :] * value[block]
                        + ratio_ref[row, :] * (value[block] - right[block])
                    )
                    product = jnp.dot(
                        jnp.concatenate(split(right[block]), axis=0), tables[block],
                        preferred_element_type=F32,
                    )
                    value[block] = product[:members, :LANES] + (
                        product[members:, :LANES] + product[:members, LANES:]
                    )
                own_ref[step, :, lanes] = value[block]
                at_inlet[step] = jnp.where(
                    member_block == block, take(value[block], member_lane), at_inlet[step]
                )
        return at_inlet

    groups = list(range(0, blocks, GROUP))
    for first in groups[:1]:
        at_inlet = solve_group(first, list(at_inlet))

    unit = jnp.where(exit_ref[...] >= 0, 1.0, 0.0).astype(F32)
    response = [unit]
    gain = [jnp.where(interior, next_new, 0.0)]
    base = jnp.where(interior, next_new * weight_stay + next_old, 0.0)
    for lag in range(1, steps):
        response.append(response[-1] * weight_stay)
        gain.append(base)
        base = base * weight_stay
    for level in range(levels_of(LANES)):
        pulled = [take(value, pointer) for value in response]
        added = multiply_series(steps, gain, pulled)
        response = [value + more for value, more in zip(response, added)]
        if level + 1 < levels_of(LANES):
            gain = multiply_series(steps, gain, [take(value, pointer) for value in gain])
        pointer = take(pointer, pointer)
    slot = take(exit_ref[...], pointer)
    slot = jnp.maximum(slot, 0)
    slot_ref[...] = slot
    for lag in range(steps):
        response_ref[lag] = response[lag]

    lane_rows = jnp.broadcast_to(inlet_lane, (blocks, LANES))
    block_rows = lax.broadcasted_iota(jnp.int32, (blocks, LANES), 0)
    chosen = block_rows == jnp.broadcast_to(inlet_block, (blocks, LANES))

    def at_inlets(rows):
        return jnp.sum(jnp.where(chosen, take(rows, lane_rows), 0.0), axis=0, keepdims=True)

    travel_in = at_inlets(travel)
    slot_in = at_inlets(slot.astype(F32))
    response_in = [at_inlets(value) for value in response]
    new_in, old_in, _ = weights_of(travel_in)

    for first in groups[1:]:
        at_inlet = solve_group(first, list(at_inlet))

    for step in range(steps):
        rows = pl.ds(step * members, members)
        inlet_values_ref[rows, :] = at_inlet[step]
        outgoing = new_in * at_inlet[step]
        if step + 1 < steps:
            outgoing = outgoing + old_in * at_inlet[step + 1]
        message_ref[rows, :] = outgoing
    tail = []
    for lag in range(steps):
        coefficient = new_in * response_in[lag]
        if lag > 0:
            coefficient = coefficient + old_in * response_in[lag - 1]
        tail.append(coefficient)
    message_ref[pl.ds(steps * members, EXTRA), :] = eight_rows(tail + [slot_in])
    inlet_rows_ref[...] = eight_rows(response_in + [travel_in, slot_in])


def eight_rows(rows):
    rows = list(rows)
    while len(rows) % EXTRA:
        rows.append(jnp.zeros_like(rows[0]))
    return jnp.concatenate(rows, axis=0)


def compose(steps, members, upper, lower):
    values, coefficients, slot = upper
    below, below_coefficients, below_slot = lower
    index = jnp.broadcast_to(slot, (members, LANES)).astype(jnp.int32)
    pulled = [take(value, index) for value in below]
    result = []
    for step in range(steps):
        total = values[step]
        for lag in range(steps - step):
            total = total + coefficients[lag] * pulled[step + lag]
        result.append(total)
    if below_coefficients is None:
        return result, None, None
    table = eight_rows(list(below_coefficients) + [below_slot])
    table = take(table, jnp.broadcast_to(slot, table.shape).astype(jnp.int32))
    combined = multiply_series(
        steps, coefficients, [table[lag:lag + 1] for lag in range(steps)]
    )
    return result, combined, table[steps:steps + 1]


def read_message(steps, members, ref):
    values = [ref[pl.ds(step * members, members), :] for step in range(steps)]
    tail = ref[pl.ds(steps * members, EXTRA), :]
    return values, [tail[lag:lag + 1] for lag in range(steps)], tail[steps:steps + 1]


def write_message(steps, members, ref, message):
    values, coefficients, slot = message
    for step in range(steps):
        ref[pl.ds(step * members, members), :] = values[step]
    ref[pl.ds(steps * members, EXTRA), :] = eight_rows(list(coefficients) + [slot])


def identity_message(steps, members):
    zero = jnp.zeros((members, LANES), F32)
    row = jnp.zeros((1, LANES), F32)
    lane = lax.broadcasted_iota(jnp.int32, (8, LANES), 1).astype(F32)[0:1]
    return [zero] * steps, [row + 1.0] + [row] * (steps - 1), lane


def digit_of(axis, stride, radix):
    return (lax.axis_index(axis) // stride) % radix


def group_kernel(steps, members, axis, stride, radix, has_inner, *refs):
    messages = refs[:radix]
    inner = refs[radix] if has_inner else None
    outs = refs[radix + has_inner:]
    digit = digit_of(axis, stride, radix)
    for mine in range(radix):
        @pl.when(digit == mine)
        def _(mine=mine):
            total = None
            later = None
            for other in reversed(range(radix)):
                message = read_message(steps, members, messages[source_of(mine, other, radix)])
                total = message if total is None else compose(steps, members, message, total)
                if other == mine + 1:
                    later = total
            if later is None:
                later = identity_message(steps, members)
            if has_inner:
                later = compose(steps, members, read_message(steps, members, inner), later)
            write_message(steps, members, outs[0], later)
            write_message(steps, members, outs[1], total)


def last_round(steps, members, axis, stride, radix, messages, inner, out):
    digit = digit_of(axis, stride, radix)
    for mine in range(radix):
        @pl.when(digit == mine)
        def _(mine=mine):
            value = [jnp.zeros((members, LANES), F32)] * steps
            for other in reversed(range(mine + 1, radix)):
                message = read_message(steps, members, messages[source_of(mine, other, radix)])
                if other == radix - 1:
                    value = message[0]
                else:
                    value = compose(steps, members, message, (value, None, None))[0]
            if inner is not None:
                within = read_message(steps, members, inner)
                if mine == radix - 1:
                    value = within[0]
                else:
                    value = compose(steps, members, within, (value, None, None))[0]
            for step in range(steps):
                out[pl.ds(step * members, members), :] = value[step]


def is_power(number):
    return number & (number - 1) == 0


def source_of(mine, other, radix):
    return mine ^ other if is_power(radix) else (other - mine) % radix


def exchange(value, axis, stride, radix, offset):
    pairs = []
    for device in range(lax.axis_size(axis)):
        digit = (device // stride) % radix
        source = digit ^ offset if is_power(radix) else (digit + offset) % radix
        pairs.append((device + (source - digit) * stride, device))
    return lax.ppermute(value, axis, pairs)


def radices_of(count):
    radices = []
    while count > 1:
        radix = next(r for r in (4, 2, 3, 5, 7, count) if count % r == 0)
        radices.append(radix)
        count //= radix
    return radices or [1]


def leaving_kernel(steps, members, blocks, flow_ref, exit_ref, leaving_ref):
    sub = lax.broadcasted_iota(jnp.int32, (LANES, LANES), 0)
    total = None
    for block in range(blocks):
        lanes = pl.ds(block * LANES, LANES)
        table = (sub == exit_ref[pl.ds(block, 1), :]).astype(F32).astype(jnp.bfloat16)
        flows = flow_ref[:, :, lanes].reshape((steps + 1) * members, LANES)
        part = lax.dot_general(
            flows, table, (((1,), (1,)), ((), ())), preferred_element_type=F32
        )
        total = part if total is None else total + part
    leaving_ref[...] = total


def weight_kernel(
    steps, members, blocks,
    flow_ref, lateral_ref, rough_ref, factor_ref, down_ref, weight_ref, slopes_ref,
):
    slopes = slopes_of(rough_ref[...] * factor_ref[...])
    for i in range(4):
        slopes_ref[i] = slopes[i]
    sub = lax.broadcasted_iota(jnp.int32, (LANES, LANES), 0)

    def one_block(block, carry):
        lanes = pl.ds(pl.multiple_of(block * LANES, LANES), LANES)
        row = pl.ds(block, 1)
        table = (sub == down_ref[row, :]).astype(F32).astype(jnp.bfloat16)
        flows = flow_ref[:, :, lanes].reshape((steps + 1) * members, LANES)
        inflow = lax.dot_general(
            flows, table, (((1,), (1,)), ((), ())), preferred_element_type=F32
        )
        new, old, stay, side = (slopes_ref[i, row, :] for i in range(4))
        for step in range(steps):
            now = inflow[(step + 1) * members:(step + 2) * members]
            prior = inflow[step * members:(step + 1) * members]
            weight_ref[step, :, lanes] = (
                new * now
                + old * prior
                + stay * flow_ref[step, :, lanes].astype(F32)
                + side * lateral_ref[step, :, lanes].astype(F32)
            )
        return carry

    lax.fori_loop(0, blocks, one_block, 0, unroll=4)


def final_kernel(steps, members, blocks, ranks, stride, radix, has_inner, *refs):
    messages, refs = refs[:radix], refs[radix:]
    inner, refs = (refs[0], refs[1:]) if has_inner else (None, refs)
    (
        own_ref, response_ref, slot_ref, weight_ref, rough_ref, factor_ref,
        inlet_values_ref, inlet_rows_ref, arriving_ref, inlet_ref,
    ) = refs[:10]
    grad_ref = refs[10]
    pieces = refs[11:11 + ranks]
    part_ref, side_ref, incoming_ref = refs[11 + ranks:]
    last_round(steps, members, "net", stride, radix, messages, inner, incoming_ref)
    travel = rough_ref[...] * factor_ref[...]
    side_ref[...] = 1.0 / (travel * (1.0 - skew_weight) + 0.5)
    shape = (members, LANES)

    def one_block(block, carry):
        place = pl.ds(pl.multiple_of(block * LANES, LANES), LANES)
        row = pl.ds(block, 1)
        index = jnp.broadcast_to(slot_ref[row, :], shape)
        response = [response_ref[lag, row, :] for lag in range(steps)]
        side = side_ref[row, :]
        pulled = [
            take(incoming_ref[pl.ds(step * members, members), :], index) for step in range(steps)
        ]
        total = jnp.zeros(shape, F32)
        for step in range(steps):
            value = own_ref[step, :, place]
            for lag in range(steps - step):
                value = value + response[lag] * pulled[step + lag]
            grad_ref[step, :, place] = (side * value).astype(jnp.bfloat16)
            total = total + value * weight_ref[step, :, place]
        part_ref[row, :] = jnp.sum(total, axis=0, keepdims=True)
        return carry

    lax.fori_loop(0, blocks, one_block, 0, unroll=4)

    rows = inlet_rows_ref[...]
    slope_new, slope_old, _, _ = slopes_of(rows[steps:steps + 1])
    index = jnp.broadcast_to(rows[steps + 1:steps + 2], shape).astype(jnp.int32)
    pulled = [
        take(incoming_ref[pl.ds(step * members, members), :], index) for step in range(steps)
    ]
    total = jnp.zeros(shape, F32)
    for step in range(steps):
        value = inlet_values_ref[pl.ds(step * members, members), :]
        for lag in range(steps - step):
            value = value + rows[lag:lag + 1] * pulled[step + lag]
        total = total + value * (
            slope_new * arriving_ref[pl.ds((step + 1) * members, members), :]
            + slope_old * arriving_ref[pl.ds(step * members, members), :]
        )
    at_inlet = jnp.sum(total, axis=0, keepdims=True)
    inlet = inlet_ref[...]
    inlet_block = inlet // LANES
    inlet_lane = inlet - inlet_block * LANES
    block_rows = lax.broadcasted_iota(jnp.int32, (blocks, LANES), 0)
    spread = jnp.where(block_rows == inlet_block, at_inlet, 0.0)
    lane_table = (
        lax.broadcasted_iota(jnp.int32, (LANES, LANES), 0)
        == jnp.broadcast_to(inlet_lane, (LANES, LANES))
    ).astype(F32)
    placed = lax.dot_general(
        spread, lane_table, (((1,), (1,)), ((), ())),
        precision=lax.Precision.HIGHEST, preferred_element_type=F32,
    )
    part_ref[...] = factor_ref[...] * (part_ref[...] + placed)
    mine = lax.axis_index("mem")
    piece = blocks // ranks
    for offset in range(ranks):
        target = mine ^ offset if is_power(ranks) else (mine + offset) % ranks
        pieces[offset][...] = part_ref[pl.ds(pl.multiple_of(target * piece, piece), piece), :]


def call(kernel, name, out_shape, scratch=(), flops=0, size=0):
    return pl.pallas_call(
        kernel,
        out_shape=out_shape,
        scratch_shapes=scratch,
        compiler_params=pltpu.CompilerParams(vmem_limit_bytes=VMEM_BYTES),
        cost_estimate=pl.CostEstimate(flops=flops, bytes_accessed=size, transcendentals=0),
        name=name,
    )


def body(
    stored_reach_flows, lateral, cotangent, roughness, travel_factor,
    inverse_block_matrix, down_in_block, exit_slot, inlet_reach,
):
    steps, members, reaches = cotangent.shape
    blocks = reaches // LANES
    count = lax.axis_size("net")
    ranks = lax.axis_size("mem")
    rough = roughness.reshape(blocks, LANES)
    factor = travel_factor.reshape(blocks, LANES)
    down = down_in_block.reshape(blocks, LANES)
    leave = exit_slot.reshape(blocks, LANES)
    rows = steps * members + EXTRA
    shape = jax.ShapeDtypeStruct
    work = steps * members * reaches

    own, message, response, slot, inlet_values, inlet_rows = call(
        functools.partial(local_kernel, steps, members, blocks),
        "local",
        (
            shape((steps, members, reaches), F32),
            shape((rows, LANES), F32),
            shape((steps, blocks, LANES), F32),
            shape((blocks, LANES), jnp.int32),
            shape((steps * members, LANES), F32),
            shape((EXTRA, LANES), F32),
        ),
        scratch=[pltpu.VMEM((blocks, LANES), F32)] * 2,
        flops=8 * LANES * work,
        size=6 * work,
    )(cotangent, inverse_block_matrix, rough, factor, down, leave, inlet_reach)

    leaving = call(
        functools.partial(leaving_kernel, steps, members, blocks),
        "leaving",
        shape(((steps + 1) * members, LANES), F32),
        flops=2 * LANES * work,
        size=2 * work,
    )(stored_reach_flows, leave)
    weight = call(
        functools.partial(weight_kernel, steps, members, blocks),
        "weight",
        shape((steps, members, reaches), F32),
        scratch=[pltpu.VMEM((4, blocks, LANES), F32)],
        flops=2 * LANES * work,
        size=8 * work,
    )(stored_reach_flows, lateral, rough, factor, down)
    arriving = lax.ppermute(leaving, "net", [(i, i + 1) for i in range(count - 1)])

    stride = 1
    inner = ()
    radices = radices_of(count)
    for radix in radices[:-1]:
        received = [message] + [
            exchange(message, "net", stride, radix, offset) for offset in range(1, radix)
        ]
        later, message = call(
            functools.partial(group_kernel, steps, members, "net", stride, radix, len(inner)),
            "compose",
            (shape((rows, LANES), F32),) * 2,
            flops=20 * radix * rows * LANES,
            size=4 * radix * rows * LANES,
        )(*received, *inner)
        inner = (later,)
        stride *= radix
    radix = radices[-1]
    received = [message] + [
        exchange(message, "net", stride, radix, offset) for offset in range(1, radix)
    ]

    piece = shape((blocks // ranks, LANES), F32)
    grad_lateral, *pieces = call(
        functools.partial(
            final_kernel, steps, members, blocks, ranks, stride, radix, len(inner)
        ),
        "finish",
        (shape((steps, members, reaches), jnp.bfloat16),) + (piece,) * ranks,
        scratch=[
            pltpu.VMEM((blocks, LANES), F32),
            pltpu.VMEM((blocks, LANES), F32),
            pltpu.VMEM((steps * members, LANES), F32),
        ],
        flops=30 * work,
        size=10 * work,
    )(
        *received, *inner, own, response, slot, weight, rough, factor,
        inlet_values, inlet_rows, arriving, inlet_reach,
    )
    total = pieces[0]
    for offset in range(1, ranks):
        back = offset if is_power(ranks) else ranks - offset
        total = total + exchange(pieces[offset], "mem", 1, ranks, back)
    return grad_lateral, total.reshape(-1)


def solution(mesh):
    in_specs = (
        P(None, "mem", "net"),
        P(None, "mem", "net"),
        P(None, "mem", "net"),
        P("net"),
        P("net"),
        P("net", None, None),
        P("net"),
        P("net"),
        P("net", None),
    )
    out_specs = (P(None, "mem", "net"), P(("net", "mem")))
    return jax.shard_map(body, mesh=mesh, in_specs=in_specs, out_specs=out_specs, check_vma=False)
```

```python
import functools

import jax
import jax.numpy as jnp
from jax import lax
from jax.experimental import pallas as pl
from jax.experimental.pallas import tpu as pltpu
from jax.sharding import PartitionSpec as P


skew_weight = 0.2
LANES = 128
EXTRA = 8
F32 = jnp.float32


ROW_GATHER = lax.GatherDimensionNumbers(
    offset_dims=(), collapsed_slice_dims=(1,), start_index_map=(1,),
    operand_batching_dims=(0,), start_indices_batching_dims=(0,),
)
VMEM_BYTES = 20 << 20
GROUP = 8


def take(values, index):
    return lax.gather(
        values, index[..., None], ROW_GATHER, (1, 1),
        mode=lax.GatherScatterMode.PROMISE_IN_BOUNDS,
    )


def weights_of(travel):
    divisor = travel * (1.0 - skew_weight) + 0.5
    weight_new = (0.5 - travel * skew_weight) / divisor
    weight_old = (0.5 + travel * skew_weight) / divisor
    weight_stay = (travel * (1.0 - skew_weight) - 0.5) / divisor
    return weight_new, weight_old, weight_stay


def slopes_of(travel):
    divisor = travel * (1.0 - skew_weight) + 0.5
    square = divisor * divisor
    return (
        -0.5 / square,
        (skew_weight - 0.5) / square,
        (1.0 - skew_weight) / square,
        (skew_weight - 1.0) / square,
    )


def levels_of(lanes):
    count = 0
    while (1 << count) < lanes:
        count += 1
    return count


def split(value):
    high = value.astype(jnp.bfloat16)
    return high, (value - high.astype(F32)).astype(jnp.bfloat16)


def multiply_series(steps, left, right):
    result = []
    for lag in range(steps):
        total = left[0] * right[lag]
        for first in range(1, lag + 1):
            total = total + left[first] * right[lag - first]
        result.append(total)
    return result


def local_kernel(
    steps, members, blocks,
    cot_hbm, matrix_hbm, rough_hbm, factor_hbm, down_hbm, exit_hbm, inlet_hbm,
    own_ref, message_ref, response_ref, slot_ref, inlet_values_ref, inlet_rows_ref,
    stay_ref, ratio_ref,
    cot_ref, matrix_ref, rough_ref, factor_ref, down_ref, exit_ref, inlet_ref,
    small_sem, cot_sem, matrix_sem,
):
    groups = list(range(0, blocks, GROUP))
    small = [
        pltpu.make_async_copy(source, target, small_sem.at[i])
        for i, (source, target) in enumerate((
            (rough_hbm, rough_ref), (factor_hbm, factor_ref), (down_hbm, down_ref),
            (exit_hbm, exit_ref), (inlet_hbm, inlet_ref),
        ))
    ]
    large = []
    for i, first in enumerate(groups):
        size = min(GROUP, blocks - first)
        lanes = pl.ds(first * LANES, size * LANES)
        large.append((
            pltpu.make_async_copy(
                matrix_hbm.at[pl.ds(first, size)], matrix_ref.at[pl.ds(first, size)], matrix_sem.at[i]
            ),
            pltpu.make_async_copy(
                cot_hbm.at[:, :, lanes], cot_ref.at[:, :, lanes], cot_sem.at[i]
            ),
        ))
    for copy in small:
        copy.start()
    for pair in large:
        for copy in pair:
            copy.start()
    for copy in small:
        copy.wait()

    travel = rough_ref[...] * factor_ref[...]
    weight_new, weight_old, weight_stay = weights_of(travel)
    down = down_ref[...]
    lane = lax.broadcasted_iota(jnp.int32, down.shape, 1)
    interior = down < LANES
    pointer = jnp.where(interior, down, lane)
    next_new = take(weight_new, pointer)
    next_old = take(weight_old, pointer)
    ratio = jnp.where(interior, next_old / next_new, 0.0)
    stay_ref[...] = weight_stay
    ratio_ref[...] = ratio

    inlet = inlet_ref[...]
    inlet_block = inlet // LANES
    inlet_lane = inlet - inlet_block * LANES
    member_lane = jnp.broadcast_to(inlet_lane, (members, LANES))
    member_block = jnp.broadcast_to(inlet_block, (members, LANES))
    at_inlet = [jnp.zeros((members, LANES), F32)] * steps

    def solve_group(first, at_inlet):
        places = range(first, min(first + GROUP, blocks))
        tables = {
            block: jnp.concatenate(split(matrix_ref[block]), axis=1) for block in places
        }
        right, value = {}, {}
        for step in reversed(range(steps)):
            for block in places:
                lanes = pl.ds(block * LANES, LANES)
                row = pl.ds(block, 1)
                source = cot_ref[step, :, lanes]
                if step == steps - 1:
                    right[block] = source.astype(F32)
                    product = jnp.dot(source, tables[block], preferred_element_type=F32)
                    value[block] = product[:, :LANES] + product[:, LANES:]
                else:
                    right[block] = (
                        source.astype(F32)
                        + stay_ref[row, :] * value[block]
                        + ratio_ref[row, :] * (value[block] - right[block])
                    )
                    product = jnp.dot(
                        jnp.concatenate(split(right[block]), axis=0), tables[block],
                        preferred_element_type=F32,
                    )
                    value[block] = product[:members, :LANES] + (
                        product[members:, :LANES] + product[:members, LANES:]
                    )
                own_ref[step, :, lanes] = value[block]
                at_inlet[step] = jnp.where(
                    member_block == block, take(value[block], member_lane), at_inlet[step]
                )
        return at_inlet

    unit = jnp.where(exit_ref[...] >= 0, 1.0, 0.0).astype(F32)
    response = [unit]
    gain = [jnp.where(interior, next_new, 0.0)]
    base = jnp.where(interior, next_new * weight_stay + next_old, 0.0)
    for _ in range(1, steps):
        response.append(response[-1] * weight_stay)
        gain.append(base)
        base = base * weight_stay
    for level in range(levels_of(LANES)):
        pulled = [take(value, pointer) for value in response]
        added = multiply_series(steps, gain, pulled)
        response = [value + more for value, more in zip(response, added)]
        if level + 1 < levels_of(LANES):
            gain = multiply_series(steps, gain, [take(value, pointer) for value in gain])
        pointer = take(pointer, pointer)
    slot = take(exit_ref[...], pointer)
    slot = jnp.maximum(slot, 0)
    slot_ref[...] = slot
    for lag in range(steps):
        response_ref[lag] = response[lag]

    lane_rows = jnp.broadcast_to(inlet_lane, (blocks, LANES))
    block_rows = lax.broadcasted_iota(jnp.int32, (blocks, LANES), 0)
    chosen = block_rows == jnp.broadcast_to(inlet_block, (blocks, LANES))

    def at_inlets(rows):
        return jnp.sum(jnp.where(chosen, take(rows, lane_rows), 0.0), axis=0, keepdims=True)

    travel_in = at_inlets(travel)
    slot_in = at_inlets(slot.astype(F32))
    response_in = [at_inlets(value) for value in response]
    new_in, old_in, _ = weights_of(travel_in)

    for first, pair in zip(groups, large):
        for copy in pair:
            copy.wait()
        at_inlet = solve_group(first, list(at_inlet))

    for step in range(steps):
        rows = pl.ds(step * members, members)
        inlet_values_ref[rows, :] = at_inlet[step]
        outgoing = new_in * at_inlet[step]
        if step + 1 < steps:
            outgoing = outgoing + old_in * at_inlet[step + 1]
        message_ref[rows, :] = outgoing
    tail = []
    for lag in range(steps):
        coefficient = new_in * response_in[lag]
        if lag > 0:
            coefficient = coefficient + old_in * response_in[lag - 1]
        tail.append(coefficient)
    message_ref[pl.ds(steps * members, EXTRA), :] = eight_rows(tail + [slot_in])
    inlet_rows_ref[...] = eight_rows(response_in + [travel_in, slot_in])


def eight_rows(rows):
    rows = list(rows)
    while len(rows) % EXTRA:
        rows.append(jnp.zeros_like(rows[0]))
    return jnp.concatenate(rows, axis=0)


def compose(steps, members, upper, lower):
    values, coefficients, slot = upper
    below, below_coefficients, below_slot = lower
    index = jnp.broadcast_to(slot, (members, LANES)).astype(jnp.int32)
    pulled = [take(value, index) for value in below]
    result = []
    for step in range(steps):
        total = values[step]
        for lag in range(steps - step):
            total = total + coefficients[lag] * pulled[step + lag]
        result.append(total)
    if below_coefficients is None:
        return result, None, None
    table = eight_rows(list(below_coefficients) + [below_slot])
    table = take(table, jnp.broadcast_to(slot, table.shape).astype(jnp.int32))
    combined = multiply_series(
        steps, coefficients, [table[lag:lag + 1] for lag in range(steps)]
    )
    return result, combined, table[steps:steps + 1]


def read_message(steps, members, ref):
    values = [ref[pl.ds(step * members, members), :] for step in range(steps)]
    tail = ref[pl.ds(steps * members, EXTRA), :]
    return values, [tail[lag:lag + 1] for lag in range(steps)], tail[steps:steps + 1]


def write_message(steps, members, ref, message):
    values, coefficients, slot = message
    for step in range(steps):
        ref[pl.ds(step * members, members), :] = values[step]
    ref[pl.ds(steps * members, EXTRA), :] = eight_rows(list(coefficients) + [slot])


def identity_message(steps, members):
    zero = jnp.zeros((members, LANES), F32)
    row = jnp.zeros((1, LANES), F32)
    lane = lax.broadcasted_iota(jnp.int32, (8, LANES), 1).astype(F32)[0:1]
    return [zero] * steps, [row + 1.0] + [row] * (steps - 1), lane


def digit_of(axis, stride, radix):
    return (lax.axis_index(axis) // stride) % radix


def group_kernel(steps, members, axis, stride, radix, has_inner, *refs):
    messages = refs[:radix]
    inner = refs[radix] if has_inner else None
    outs = refs[radix + has_inner:]
    digit = digit_of(axis, stride, radix)
    for mine in range(radix):
        @pl.when(digit == mine)
        def _(mine=mine):
            total = None
            later = None
            for other in reversed(range(radix)):
                message = read_message(steps, members, messages[source_of(mine, other, radix)])
                total = message if total is None else compose(steps, members, message, total)
                if other == mine + 1:
                    later = total
            if later is None:
                later = identity_message(steps, members)
            if has_inner:
                later = compose(steps, members, read_message(steps, members, inner), later)
            write_message(steps, members, outs[0], later)
            write_message(steps, members, outs[1], total)


def last_round(steps, members, axis, stride, radix, messages, inner, out):
    digit = digit_of(axis, stride, radix)
    for mine in range(radix):
        @pl.when(digit == mine)
        def _(mine=mine):
            value = [jnp.zeros((members, LANES), F32)] * steps
            for other in reversed(range(mine + 1, radix)):
                message = read_message(steps, members, messages[source_of(mine, other, radix)])
                if other == radix - 1:
                    value = message[0]
                else:
                    value = compose(steps, members, message, (value, None, None))[0]
            if inner is not None:
                within = read_message(steps, members, inner)
                if mine == radix - 1:
                    value = within[0]
                else:
                    value = compose(steps, members, within, (value, None, None))[0]
            for step in range(steps):
                out[pl.ds(step * members, members), :] = value[step]


def is_power(number):
    return number & (number - 1) == 0


def source_of(mine, other, radix):
    return mine ^ other if is_power(radix) else (other - mine) % radix


def exchange(value, axis, stride, radix, offset):
    pairs = []
    for device in range(lax.axis_size(axis)):
        digit = (device // stride) % radix
        source = digit ^ offset if is_power(radix) else (digit + offset) % radix
        pairs.append((device + (source - digit) * stride, device))
    return lax.ppermute(value, axis, pairs)


def radices_of(count):
    radices = []
    while count > 1:
        radix = next(r for r in (4, 2, 3, 5, 7, count) if count % r == 0)
        radices.append(radix)
        count //= radix
    return radices or [1]


def leaving_kernel(steps, members, blocks, flow_ref, exit_ref, leaving_ref):
    sub = lax.broadcasted_iota(jnp.int32, (LANES, LANES), 0)
    total = None
    for block in range(blocks):
        lanes = pl.ds(block * LANES, LANES)
        table = (sub == exit_ref[pl.ds(block, 1), :]).astype(F32).astype(jnp.bfloat16)
        flows = flow_ref[:, :, lanes].reshape((steps + 1) * members, LANES)
        part = lax.dot_general(
            flows, table, (((1,), (1,)), ((), ())), preferred_element_type=F32
        )
        total = part if total is None else total + part
    leaving_ref[...] = total


def weight_kernel(
    steps, members, blocks,
    flow_ref, lateral_ref, own_ref, rough_ref, factor_ref, down_ref,
    weight_ref, part_ref, slopes_ref,
):
    slopes = slopes_of(rough_ref[...] * factor_ref[...])
    for i in range(4):
        slopes_ref[i] = slopes[i]
    sub = lax.broadcasted_iota(jnp.int32, (LANES, LANES), 0)

    def one_block(block, carry):
        lanes = pl.ds(pl.multiple_of(block * LANES, LANES), LANES)
        row = pl.ds(block, 1)
        table = (sub == down_ref[row, :]).astype(F32).astype(jnp.bfloat16)
        flows = flow_ref[:, :, lanes].reshape((steps + 1) * members, LANES)
        inflow = lax.dot_general(
            flows, table, (((1,), (1,)), ((), ())), preferred_element_type=F32
        )
        new, old, stay, side = (slopes_ref[i, row, :] for i in range(4))
        total = jnp.zeros((members, LANES), F32)
        for step in range(steps):
            now = inflow[(step + 1) * members:(step + 2) * members]
            prior = inflow[step * members:(step + 1) * members]
            weight = (
                new * now
                + old * prior
                + stay * flow_ref[step, :, lanes].astype(F32)
                + side * lateral_ref[step, :, lanes].astype(F32)
            )
            weight_ref[step, :, lanes] = weight
            total = total + weight * own_ref[step, :, lanes]
        part_ref[row, :] = jnp.sum(total, axis=0, keepdims=True)
        return carry

    lax.fori_loop(0, blocks, one_block, 0, unroll=4)


def sums_kernel(steps, members, blocks, ranks, stride, radix, has_inner, *refs):
    messages, refs = refs[:radix], refs[radix:]
    inner, refs = (refs[0], refs[1:]) if has_inner else (None, refs)
    (
        response_ref, slot_ref, weight_ref, own_part_ref, factor_ref,
        inlet_values_ref, inlet_rows_ref, arriving_ref, inlet_ref,
    ) = refs[:9]
    incoming_ref = refs[9]
    pieces = refs[10:10 + ranks]
    (part_ref,) = refs[10 + ranks:]
    last_round(steps, members, "net", stride, radix, messages, inner, incoming_ref)
    shape = (members, LANES)

    def one_block(block, carry):
        lanes = pl.ds(pl.multiple_of(block * LANES, LANES), LANES)
        row = pl.ds(block, 1)
        index = jnp.broadcast_to(slot_ref[row, :], shape)
        pulled = [
            take(incoming_ref[pl.ds(step * members, members), :], index) for step in range(steps)
        ]
        weight = [weight_ref[step, :, lanes] for step in range(steps)]
        total = None
        for lag in range(steps):
            inside = pulled[lag] * weight[0]
            for step in range(1, steps - lag):
                inside = inside + pulled[step + lag] * weight[step]
            inside = response_ref[lag, row, :] * inside
            total = inside if total is None else total + inside
        part_ref[row, :] = own_part_ref[row, :] + jnp.sum(total, axis=0, keepdims=True)
        return carry

    lax.fori_loop(0, blocks, one_block, 0, unroll=4)

    rows = inlet_rows_ref[...]
    slope_new, slope_old, _, _ = slopes_of(rows[steps:steps + 1])
    index = jnp.broadcast_to(rows[steps + 1:steps + 2], shape).astype(jnp.int32)
    pulled = [
        take(incoming_ref[pl.ds(step * members, members), :], index) for step in range(steps)
    ]
    total = jnp.zeros(shape, F32)
    for step in range(steps):
        value = inlet_values_ref[pl.ds(step * members, members), :]
        for lag in range(steps - step):
            value = value + rows[lag:lag + 1] * pulled[step + lag]
        total = total + value * (
            slope_new * arriving_ref[pl.ds((step + 1) * members, members), :]
            + slope_old * arriving_ref[pl.ds(step * members, members), :]
        )
    at_inlet = jnp.sum(total, axis=0, keepdims=True)
    inlet = inlet_ref[...]
    inlet_block = inlet // LANES
    inlet_lane = inlet - inlet_block * LANES
    block_rows = lax.broadcasted_iota(jnp.int32, (blocks, LANES), 0)
    spread = jnp.where(block_rows == inlet_block, at_inlet, 0.0)
    lane_table = (
        lax.broadcasted_iota(jnp.int32, (LANES, LANES), 0)
        == jnp.broadcast_to(inlet_lane, (LANES, LANES))
    ).astype(F32)
    placed = lax.dot_general(
        spread, lane_table, (((1,), (1,)), ((), ())),
        precision=lax.Precision.HIGHEST, preferred_element_type=F32,
    )
    part_ref[...] = factor_ref[...] * (part_ref[...] + placed)
    mine = lax.axis_index("mem")
    piece = blocks // ranks
    for offset in range(ranks):
        target = mine ^ offset if is_power(ranks) else (mine + offset) % ranks
        pieces[offset][...] = part_ref[pl.ds(pl.multiple_of(target * piece, piece), piece), :]


def grad_kernel(
    steps, members, blocks,
    incoming_ref, own_ref, response_ref, slot_ref, rough_ref, factor_ref, grad_ref, side_ref,
):
    side_ref[...] = 1.0 / (rough_ref[...] * factor_ref[...] * (1.0 - skew_weight) + 0.5)
    shape = (members, LANES)

    def one_block(block, carry):
        lanes = pl.ds(pl.multiple_of(block * LANES, LANES), LANES)
        row = pl.ds(block, 1)
        index = jnp.broadcast_to(slot_ref[row, :], shape)
        pulled = [
            take(incoming_ref[pl.ds(step * members, members), :], index) for step in range(steps)
        ]
        for step in range(steps):
            value = own_ref[step, :, lanes]
            for lag in range(steps - step):
                value = value + response_ref[lag, row, :] * pulled[step + lag]
            grad_ref[step, :, lanes] = (side_ref[row, :] * value).astype(jnp.bfloat16)
        return carry

    lax.fori_loop(0, blocks, one_block, 0, unroll=4)


def call(kernel, out_shape, scratch=(), flops=0, size=0, **specs):
    return pl.pallas_call(
        kernel,
        out_shape=out_shape,
        **specs,
        scratch_shapes=scratch,
        compiler_params=pltpu.CompilerParams(vmem_limit_bytes=VMEM_BYTES),
        cost_estimate=pl.CostEstimate(flops=flops, bytes_accessed=size, transcendentals=0),
    )


def gradients(
    stored_reach_flows, lateral, cotangent, roughness, travel_factor,
    inverse_block_matrix, down_in_block, exit_slot, inlet_reach,
):
    steps, members, reaches = cotangent.shape
    blocks = reaches // LANES
    count = lax.axis_size("net")
    ranks = lax.axis_size("mem")
    rough = roughness.reshape(blocks, LANES)
    factor = travel_factor.reshape(blocks, LANES)
    down = down_in_block.reshape(blocks, LANES)
    leave = exit_slot.reshape(blocks, LANES)
    rows = steps * members + EXTRA
    shape = jax.ShapeDtypeStruct
    work = steps * members * reaches

    inputs = [
        pltpu.with_memory_space_constraint(array, pltpu.HBM)
        for array in (
            cotangent, inverse_block_matrix, rough, factor, down, leave, inlet_reach
        )
    ]
    turns = -(-blocks // GROUP)
    own, message, response, slot, inlet_values, inlet_rows = call(
        functools.partial(local_kernel, steps, members, blocks),
        (
            shape((steps, members, reaches), F32),
            shape((rows, LANES), F32),
            shape((steps, blocks, LANES), F32),
            shape((blocks, LANES), jnp.int32),
            shape((steps * members, LANES), F32),
            shape((EXTRA, LANES), F32),
        ),
        scratch=[pltpu.VMEM((blocks, LANES), F32)] * 2 + [
            pltpu.VMEM(array.shape, array.dtype) for array in inputs
        ] + [
            pltpu.SemaphoreType.DMA((5,)),
            pltpu.SemaphoreType.DMA((turns,)),
            pltpu.SemaphoreType.DMA((turns,)),
        ],
        flops=8 * LANES * work,
        size=6 * work,
        in_specs=[pl.BlockSpec(memory_space=pltpu.HBM)] * len(inputs),
    )(*inputs)
    stored_reach_flows, lateral, message = lax.optimization_barrier(
        (stored_reach_flows, lateral, message)
    )

    leaving = call(
        functools.partial(leaving_kernel, steps, members, blocks),
        shape(((steps + 1) * members, LANES), F32),
        flops=2 * LANES * work,
        size=2 * work,
    )(stored_reach_flows, leave)
    weight, own_part = call(
        functools.partial(weight_kernel, steps, members, blocks),
        (shape((steps, members, reaches), F32), shape((blocks, LANES), F32)),
        scratch=[pltpu.VMEM((4, blocks, LANES), F32)],
        flops=2 * LANES * work,
        size=8 * work,
    )(stored_reach_flows, lateral, own, rough, factor, down)

    stride = 1
    inner = ()
    radices = radices_of(count)
    for turn, radix in enumerate(radices[:-1]):
        received = [
            exchange(message, "net", stride, radix, offset) for offset in range(1, radix)
        ]
        if turn == 0:
            message, leaving, weight = lax.optimization_barrier((message, leaving, weight))
        received = [message] + received
        later, message = call(
            functools.partial(group_kernel, steps, members, "net", stride, radix, len(inner)),
            (shape((rows, LANES), F32),) * 2,
            flops=20 * radix * rows * LANES,
            size=4 * radix * rows * LANES,
        )(*received, *inner)
        inner = (later,)
        stride *= radix
    radix = radices[-1]
    message, leaving = lax.optimization_barrier((message, leaving))
    received = [message] + [
        exchange(message, "net", stride, radix, offset) for offset in range(1, radix)
    ]
    arriving = lax.ppermute(leaving, "net", [(i, i + 1) for i in range(count - 1)])

    piece = shape((blocks // ranks, LANES), F32)
    incoming, *pieces = call(
        functools.partial(
            sums_kernel, steps, members, blocks, ranks, stride, radix, len(inner)
        ),
        (shape((steps * members, LANES), F32),) + (piece,) * ranks,
        scratch=[pltpu.VMEM((blocks, LANES), F32)],
        flops=20 * work,
        size=4 * work,
    )(
        *received, *inner, response, slot, weight, own_part, factor,
        inlet_values, inlet_rows, arriving, inlet_reach,
    )
    grad_lateral = call(
        functools.partial(grad_kernel, steps, members, blocks),
        shape((steps, members, reaches), jnp.bfloat16),
        scratch=[pltpu.VMEM((blocks, LANES), F32)],
        flops=30 * work,
        size=6 * work,
    )(incoming, own, response, slot, rough, factor)
    total = pieces[0]
    for offset in range(1, ranks):
        back = offset if is_power(ranks) else ranks - offset
        total = total + exchange(pieces[offset], "mem", 1, ranks, back)
    return grad_lateral, total.reshape(-1)


def solution(mesh):
    in_specs = (
        P(None, "mem", "net"),
        P(None, "mem", "net"),
        P(None, "mem", "net"),
        P("net"),
        P("net"),
        P("net", None, None),
        P("net"),
        P("net"),
        P("net", None),
    )
    out_specs = (P(None, "mem", "net"), P(("net", "mem")))
    return jax.shard_map(gradients, mesh=mesh, in_specs=in_specs, out_specs=out_specs, check_vma=False)
```

```python
import functools

import jax
import jax.numpy as jnp
from jax import lax
from jax.experimental import pallas as pl
from jax.experimental.pallas import tpu as pltpu
from jax.sharding import PartitionSpec as P


skew_weight = 0.2
LANES = 128
EXTRA = 8
F32 = jnp.float32


ROW_GATHER = lax.GatherDimensionNumbers(
    offset_dims=(), collapsed_slice_dims=(1,), start_index_map=(1,),
    operand_batching_dims=(0,), start_indices_batching_dims=(0,),
)
VMEM_BYTES = 20 << 20
GROUP = 8


def take(values, index):
    return lax.gather(
        values, index[..., None], ROW_GATHER, (1, 1),
        mode=lax.GatherScatterMode.PROMISE_IN_BOUNDS,
    )


def weights_of(travel):
    divisor = travel * (1.0 - skew_weight) + 0.5
    weight_new = (0.5 - travel * skew_weight) / divisor
    weight_old = (0.5 + travel * skew_weight) / divisor
    weight_stay = (travel * (1.0 - skew_weight) - 0.5) / divisor
    return weight_new, weight_old, weight_stay


def slopes_of(travel):
    divisor = travel * (1.0 - skew_weight) + 0.5
    square = divisor * divisor
    return (
        -0.5 / square,
        (skew_weight - 0.5) / square,
        (1.0 - skew_weight) / square,
        (skew_weight - 1.0) / square,
    )


def levels_of(lanes):
    count = 0
    while (1 << count) < lanes:
        count += 1
    return count


def split(value):
    high = value.astype(jnp.bfloat16)
    return high, (value - high.astype(F32)).astype(jnp.bfloat16)


def multiply_series(steps, left, right):
    result = []
    for lag in range(steps):
        total = left[0] * right[lag]
        for first in range(1, lag + 1):
            total = total + left[first] * right[lag - first]
        result.append(total)
    return result


def local_kernel(
    steps, members, blocks,
    cot_ref, matrix_ref, rough_ref, factor_ref, down_ref, exit_ref, inlet_ref, lateral_hbm,
    own_ref, message_ref, response_ref, slot_ref, inlet_values_ref, inlet_rows_ref, lateral_ref,
    stay_ref, ratio_ref, lateral_sem,
):
    lateral_copy = pltpu.make_async_copy(lateral_hbm, lateral_ref, lateral_sem)
    lateral_copy.start()

    travel = rough_ref[...] * factor_ref[...]
    weight_new, weight_old, weight_stay = weights_of(travel)
    down = down_ref[...]
    lane = lax.broadcasted_iota(jnp.int32, down.shape, 1)
    interior = down < LANES
    pointer = jnp.where(interior, down, lane)
    next_new = take(weight_new, pointer)
    next_old = take(weight_old, pointer)
    ratio = jnp.where(interior, next_old / next_new, 0.0)
    stay_ref[...] = weight_stay
    ratio_ref[...] = ratio

    inlet = inlet_ref[...]
    inlet_block = inlet // LANES
    inlet_lane = inlet - inlet_block * LANES
    member_lane = jnp.broadcast_to(inlet_lane, (members, LANES))
    member_block = jnp.broadcast_to(inlet_block, (members, LANES))
    at_inlet = [jnp.zeros((members, LANES), F32)] * steps

    def solve_group(first, at_inlet):
        places = range(first, min(first + GROUP, blocks))
        tables = {
            block: jnp.concatenate(split(matrix_ref[block]), axis=1) for block in places
        }
        right, value = {}, {}
        for step in reversed(range(steps)):
            for block in places:
                lanes = pl.ds(block * LANES, LANES)
                row = pl.ds(block, 1)
                source = cot_ref[step, :, lanes]
                if step == steps - 1:
                    right[block] = source.astype(F32)
                    product = jnp.dot(source, tables[block], preferred_element_type=F32)
                    value[block] = product[:, :LANES] + product[:, LANES:]
                else:
                    right[block] = (
                        source.astype(F32)
                        + stay_ref[row, :] * value[block]
                        + ratio_ref[row, :] * (value[block] - right[block])
                    )
                    product = jnp.dot(
                        jnp.concatenate(split(right[block]), axis=0), tables[block],
                        preferred_element_type=F32,
                    )
                    value[block] = product[:members, :LANES] + (
                        product[members:, :LANES] + product[:members, LANES:]
                    )
                own_ref[step, :, lanes] = value[block]
                at_inlet[step] = jnp.where(
                    member_block == block, take(value[block], member_lane), at_inlet[step]
                )
        return at_inlet

    unit = jnp.where(exit_ref[...] >= 0, 1.0, 0.0).astype(F32)
    response = [unit]
    gain = [jnp.where(interior, next_new, 0.0)]
    base = jnp.where(interior, next_new * weight_stay + next_old, 0.0)
    for _ in range(1, steps):
        response.append(response[-1] * weight_stay)
        gain.append(base)
        base = base * weight_stay
    for level in range(levels_of(LANES)):
        pulled = [take(value, pointer) for value in response]
        added = multiply_series(steps, gain, pulled)
        response = [value + more for value, more in zip(response, added)]
        if level + 1 < levels_of(LANES):
            gain = multiply_series(steps, gain, [take(value, pointer) for value in gain])
        pointer = take(pointer, pointer)
    slot = take(exit_ref[...], pointer)
    slot = jnp.maximum(slot, 0)
    slot_ref[...] = slot
    for lag in range(steps):
        response_ref[lag] = response[lag]

    lane_rows = jnp.broadcast_to(inlet_lane, (blocks, LANES))
    block_rows = lax.broadcasted_iota(jnp.int32, (blocks, LANES), 0)
    chosen = block_rows == jnp.broadcast_to(inlet_block, (blocks, LANES))

    def at_inlets(rows):
        return jnp.sum(jnp.where(chosen, take(rows, lane_rows), 0.0), axis=0, keepdims=True)

    travel_in = at_inlets(travel)
    slot_in = at_inlets(slot.astype(F32))
    response_in = [at_inlets(value) for value in response]
    new_in, old_in, _ = weights_of(travel_in)

    for first in range(0, blocks, GROUP):
        at_inlet = solve_group(first, list(at_inlet))

    for step in range(steps):
        rows = pl.ds(step * members, members)
        inlet_values_ref[rows, :] = at_inlet[step]
        outgoing = new_in * at_inlet[step]
        if step + 1 < steps:
            outgoing = outgoing + old_in * at_inlet[step + 1]
        message_ref[rows, :] = outgoing
    tail = []
    for lag in range(steps):
        coefficient = new_in * response_in[lag]
        if lag > 0:
            coefficient = coefficient + old_in * response_in[lag - 1]
        tail.append(coefficient)
    message_ref[pl.ds(steps * members, EXTRA), :] = eight_rows(tail + [slot_in])
    inlet_rows_ref[...] = eight_rows(response_in + [travel_in, slot_in])
    lateral_copy.wait()


def eight_rows(rows):
    rows = list(rows)
    while len(rows) % EXTRA:
        rows.append(jnp.zeros_like(rows[0]))
    return jnp.concatenate(rows, axis=0)


def compose(steps, members, upper, lower):
    values, coefficients, slot = upper
    below, below_coefficients, below_slot = lower
    index = jnp.broadcast_to(slot, (members, LANES)).astype(jnp.int32)
    pulled = [take(value, index) for value in below]
    result = []
    for step in range(steps):
        total = values[step]
        for lag in range(steps - step):
            total = total + coefficients[lag] * pulled[step + lag]
        result.append(total)
    if below_coefficients is None:
        return result, None, None
    table = eight_rows(list(below_coefficients) + [below_slot])
    table = take(table, jnp.broadcast_to(slot, table.shape).astype(jnp.int32))
    combined = multiply_series(
        steps, coefficients, [table[lag:lag + 1] for lag in range(steps)]
    )
    return result, combined, table[steps:steps + 1]


def read_message(steps, members, ref):
    values = [ref[pl.ds(step * members, members), :] for step in range(steps)]
    tail = ref[pl.ds(steps * members, EXTRA), :]
    return values, [tail[lag:lag + 1] for lag in range(steps)], tail[steps:steps + 1]


def write_message(steps, members, ref, message):
    values, coefficients, slot = message
    for step in range(steps):
        ref[pl.ds(step * members, members), :] = values[step]
    ref[pl.ds(steps * members, EXTRA), :] = eight_rows(list(coefficients) + [slot])


def identity_message(steps, members):
    zero = jnp.zeros((members, LANES), F32)
    row = jnp.zeros((1, LANES), F32)
    lane = lax.broadcasted_iota(jnp.int32, (8, LANES), 1).astype(F32)[0:1]
    return [zero] * steps, [row + 1.0] + [row] * (steps - 1), lane


def digit_of(axis, stride, radix):
    return (lax.axis_index(axis) // stride) % radix


def group_kernel(steps, members, axis, stride, radix, has_inner, *refs):
    messages = refs[:radix]
    inner = refs[radix] if has_inner else None
    outs = refs[radix + has_inner:]
    digit = digit_of(axis, stride, radix)
    for mine in range(radix):
        @pl.when(digit == mine)
        def _(mine=mine):
            total = None
            later = None
            for other in reversed(range(radix)):
                message = read_message(steps, members, messages[source_of(mine, other, radix)])
                total = message if total is None else compose(steps, members, message, total)
                if other == mine + 1:
                    later = total
            if later is None:
                later = identity_message(steps, members)
            if has_inner:
                later = compose(steps, members, read_message(steps, members, inner), later)
            write_message(steps, members, outs[0], later)
            write_message(steps, members, outs[1], total)


def last_round(steps, members, axis, stride, radix, messages, inner, out):
    digit = digit_of(axis, stride, radix)
    for mine in range(radix):
        @pl.when(digit == mine)
        def _(mine=mine):
            value = [jnp.zeros((members, LANES), F32)] * steps
            for other in reversed(range(mine + 1, radix)):
                message = read_message(steps, members, messages[source_of(mine, other, radix)])
                if other == radix - 1:
                    value = message[0]
                else:
                    value = compose(steps, members, message, (value, None, None))[0]
            if inner is not None:
                within = read_message(steps, members, inner)
                if mine == radix - 1:
                    value = within[0]
                else:
                    value = compose(steps, members, within, (value, None, None))[0]
            for step in range(steps):
                out[pl.ds(step * members, members), :] = value[step]


def is_power(number):
    return number & (number - 1) == 0


def source_of(mine, other, radix):
    return mine ^ other if is_power(radix) else (other - mine) % radix


def exchange(value, axis, stride, radix, offset):
    pairs = []
    for device in range(lax.axis_size(axis)):
        digit = (device // stride) % radix
        source = digit ^ offset if is_power(radix) else (digit + offset) % radix
        pairs.append((device + (source - digit) * stride, device))
    return lax.ppermute(value, axis, pairs)


def radices_of(count):
    radices = []
    while count > 1:
        radix = next(r for r in (4, 2, 3, 5, 7, count) if count % r == 0)
        radices.append(radix)
        count //= radix
    return radices or [1]


def fetch_kernel(steps, members, blocks, count, *refs):
    sources, targets = refs[:count], refs[count:2 * count]
    leaving_ref, flow_sem, sem = refs[2 * count:]
    flow_hbm, flow_ref = sources[0], targets[0]
    exit_ref = targets[1]
    flow_copies = []
    for turn, first in enumerate(range(0, blocks, GROUP)):
        lanes = pl.ds(first * LANES, min(GROUP, blocks - first) * LANES)
        flow_copies.append(pltpu.make_async_copy(
            flow_hbm.at[:, :, lanes], flow_ref.at[:, :, lanes], flow_sem.at[turn]
        ))
    copies = [
        pltpu.make_async_copy(sources[i], targets[i], sem.at[i]) for i in range(1, count)
    ]
    copies[0].start()
    for copy in flow_copies:
        copy.start()
    for copy in copies[1:]:
        copy.start()
    copies[0].wait()
    sub = lax.broadcasted_iota(jnp.int32, (LANES, LANES), 0)
    total = None
    for block in range(blocks):
        if block % GROUP == 0:
            flow_copies[block // GROUP].wait()
        lanes = pl.ds(block * LANES, LANES)
        table = (sub == exit_ref[pl.ds(block, 1), :]).astype(F32).astype(jnp.bfloat16)
        flows = flow_ref[:, :, lanes].reshape((steps + 1) * members, LANES)
        part = lax.dot_general(
            flows, table, (((1,), (1,)), ((), ())), preferred_element_type=F32
        )
        total = part if total is None else total + part
    leaving_ref[...] = total
    for copy in copies[1:]:
        copy.wait()


def weight_kernel(
    steps, members, blocks,
    flow_ref, lateral_ref, own_ref, response_ref, rough_ref, factor_ref, down_ref,
    weight_ref, part_ref, slopes_ref,
):
    slopes = slopes_of(rough_ref[...] * factor_ref[...])
    for i in range(4):
        slopes_ref[i] = slopes[i]
    sub = lax.broadcasted_iota(jnp.int32, (LANES, LANES), 0)

    def one_block(block, carry):
        lanes = pl.ds(pl.multiple_of(block * LANES, LANES), LANES)
        row = pl.ds(block, 1)
        table = (sub == down_ref[row, :]).astype(F32).astype(jnp.bfloat16)
        flows = flow_ref[:, :, lanes].reshape((steps + 1) * members, LANES)
        inflow = lax.dot_general(
            flows, table, (((1,), (1,)), ((), ())), preferred_element_type=F32
        )
        new, old, stay, side = (slopes_ref[i, row, :] for i in range(4))
        total = jnp.zeros((members, LANES), F32)
        weights = []
        for step in range(steps):
            now = inflow[(step + 1) * members:(step + 2) * members]
            prior = inflow[step * members:(step + 1) * members]
            weight = (
                new * now
                + old * prior
                + stay * flow_ref[step, :, lanes].astype(F32)
                + side * lateral_ref[step, :, lanes].astype(F32)
            )
            weights.append(weight)
            total = total + weight * own_ref[step, :, lanes]
            folded = response_ref[0, row, :] * weight
            for lag in range(1, step + 1):
                folded = folded + response_ref[lag, row, :] * weights[step - lag]
            weight_ref[step, :, lanes] = folded
        part_ref[row, :] = jnp.sum(total, axis=0, keepdims=True)
        return carry

    lax.fori_loop(0, blocks, one_block, 0, unroll=8)


def sums_kernel(steps, members, blocks, ranks, stride, radix, has_inner, *refs):
    messages, refs = refs[:radix], refs[radix:]
    inner, refs = (refs[0], refs[1:]) if has_inner else (None, refs)
    (
        slot_ref, weight_ref, own_part_ref, factor_ref,
        inlet_values_ref, inlet_rows_ref, arriving_ref, inlet_ref,
    ) = refs[:8]
    incoming_ref = refs[8]
    pieces = refs[9:9 + ranks]
    (part_ref,) = refs[9 + ranks:]
    last_round(steps, members, "net", stride, radix, messages, inner, incoming_ref)
    shape = (members, LANES)

    def one_block(block, carry):
        lanes = pl.ds(pl.multiple_of(block * LANES, LANES), LANES)
        row = pl.ds(block, 1)
        index = jnp.broadcast_to(slot_ref[row, :], shape)
        pulled = [
            take(incoming_ref[pl.ds(step * members, members), :], index) for step in range(steps)
        ]
        total = pulled[0] * weight_ref[0, :, lanes]
        for step in range(1, steps):
            total = total + pulled[step] * weight_ref[step, :, lanes]
        part_ref[row, :] = own_part_ref[row, :] + jnp.sum(total, axis=0, keepdims=True)
        return carry

    lax.fori_loop(0, blocks, one_block, 0, unroll=16)

    rows = inlet_rows_ref[...]
    slope_new, slope_old, _, _ = slopes_of(rows[steps:steps + 1])
    index = jnp.broadcast_to(rows[steps + 1:steps + 2], shape).astype(jnp.int32)
    pulled = [
        take(incoming_ref[pl.ds(step * members, members), :], index) for step in range(steps)
    ]
    total = jnp.zeros(shape, F32)
    for step in range(steps):
        value = inlet_values_ref[pl.ds(step * members, members), :]
        for lag in range(steps - step):
            value = value + rows[lag:lag + 1] * pulled[step + lag]
        total = total + value * (
            slope_new * arriving_ref[pl.ds((step + 1) * members, members), :]
            + slope_old * arriving_ref[pl.ds(step * members, members), :]
        )
    at_inlet = jnp.sum(total, axis=0, keepdims=True)
    inlet = inlet_ref[...]
    inlet_block = inlet // LANES
    inlet_lane = inlet - inlet_block * LANES
    block_rows = lax.broadcasted_iota(jnp.int32, (blocks, LANES), 0)
    spread = jnp.where(block_rows == inlet_block, at_inlet, 0.0)
    lane_table = (
        lax.broadcasted_iota(jnp.int32, (LANES, LANES), 0)
        == jnp.broadcast_to(inlet_lane, (LANES, LANES))
    ).astype(F32)
    placed = lax.dot_general(
        spread, lane_table, (((1,), (1,)), ((), ())),
        precision=lax.Precision.HIGHEST, preferred_element_type=F32,
    )
    part_ref[...] = factor_ref[...] * (part_ref[...] + placed)
    mine = lax.axis_index("mem")
    piece = blocks // ranks
    for offset in range(ranks):
        target = mine ^ offset if is_power(ranks) else (mine + offset) % ranks
        pieces[offset][...] = part_ref[pl.ds(pl.multiple_of(target * piece, piece), piece), :]


def grad_kernel(
    steps, members, blocks, chunks,
    incoming_ref, own_ref, response_ref, slot_ref, rough_ref, factor_ref,
    grad_hbm, grad_ref, side_ref, sem,
):
    side_ref[...] = 1.0 / (rough_ref[...] * factor_ref[...] * (1.0 - skew_weight) + 0.5)
    shape = (members, LANES)
    part = blocks // chunks

    def one_block(block, carry):
        lanes = pl.ds(pl.multiple_of(block * LANES, LANES), LANES)
        row = pl.ds(block, 1)
        index = jnp.broadcast_to(slot_ref[row, :], shape)
        pulled = [
            take(incoming_ref[pl.ds(step * members, members), :], index) for step in range(steps)
        ]
        for step in range(steps):
            value = own_ref[step, :, lanes]
            for lag in range(steps - step):
                value = value + response_ref[lag, row, :] * pulled[step + lag]
            grad_ref[step, :, lanes] = (side_ref[row, :] * value).astype(jnp.bfloat16)
        return carry

    copies = []
    for chunk in range(chunks):
        lax.fori_loop(chunk * part, (chunk + 1) * part, one_block, 0, unroll=8)
        lanes = pl.ds(chunk * part * LANES, part * LANES)
        copies.append(pltpu.make_async_copy(
            grad_ref.at[:, :, lanes], grad_hbm.at[:, :, lanes], sem.at[chunk]
        ))
        copies[-1].start()
    for copy in copies:
        copy.wait()


def call(kernel, out_shape, scratch=(), flops=0, size=0, **specs):
    return pl.pallas_call(
        kernel,
        out_shape=out_shape,
        **specs,
        scratch_shapes=scratch,
        compiler_params=pltpu.CompilerParams(vmem_limit_bytes=VMEM_BYTES),
        cost_estimate=pl.CostEstimate(flops=flops, bytes_accessed=size, transcendentals=0),
    )


def gradients(
    stored_reach_flows, lateral, cotangent, roughness, travel_factor,
    inverse_block_matrix, down_in_block, exit_slot, inlet_reach,
):
    steps, members, reaches = cotangent.shape
    blocks = reaches // LANES
    count = lax.axis_size("net")
    ranks = lax.axis_size("mem")
    rough = roughness.reshape(blocks, LANES)
    factor = travel_factor.reshape(blocks, LANES)
    down = down_in_block.reshape(blocks, LANES)
    leave = exit_slot.reshape(blocks, LANES)
    rows = steps * members + EXTRA
    shape = jax.ShapeDtypeStruct
    work = steps * members * reaches

    hbm = pl.BlockSpec(memory_space=pltpu.HBM)

    def stay_out(array):
        return pltpu.with_memory_space_constraint(array, pltpu.HBM)

    inputs = (
        stored_reach_flows, leave, rough, factor, down, inlet_reach, inverse_block_matrix, cotangent
    )
    flows, leave, rough, factor, down, inlets, matrix, cotangent, leaving = call(
        functools.partial(fetch_kernel, steps, members, blocks, len(inputs)),
        tuple(shape(array.shape, array.dtype) for array in inputs)
        + (shape(((steps + 1) * members, LANES), F32),),
        scratch=[
            pltpu.SemaphoreType.DMA((-(-blocks // GROUP),)),
            pltpu.SemaphoreType.DMA((len(inputs),)),
        ],
        flops=2 * LANES * work,
        size=9 * work,
        in_specs=[hbm] * len(inputs),
    )(*(stay_out(array) for array in inputs))
    arriving = lax.ppermute(leaving, "net", [(i, i + 1) for i in range(count - 1)])

    own, message, response, slot, inlet_values, inlet_rows, lateral = call(
        functools.partial(local_kernel, steps, members, blocks),
        (
            shape((steps, members, reaches), F32),
            shape((rows, LANES), F32),
            shape((steps, blocks, LANES), F32),
            shape((blocks, LANES), jnp.int32),
            shape((steps * members, LANES), F32),
            shape((EXTRA, LANES), F32),
            shape(lateral.shape, lateral.dtype),
        ),
        scratch=[pltpu.VMEM((blocks, LANES), F32)] * 2 + [pltpu.SemaphoreType.DMA],
        flops=8 * LANES * work,
        size=6 * work,
        in_specs=[pl.BlockSpec()] * 7 + [hbm],
    )(cotangent, matrix, rough, factor, down, leave, inlets, stay_out(lateral))

    weight, own_part = call(
        functools.partial(weight_kernel, steps, members, blocks),
        (shape((steps, members, reaches), F32), shape((blocks, LANES), F32)),
        scratch=[pltpu.VMEM((4, blocks, LANES), F32)],
        flops=2 * LANES * work,
        size=8 * work,
    )(flows, lateral, own, response, rough, factor, down)

    stride = 1
    inner = ()
    radices = radices_of(count)
    for turn, radix in enumerate(radices[:-1]):
        received = [
            exchange(message, "net", stride, radix, offset) for offset in range(1, radix)
        ]
        if turn == 0:
            message, weight = lax.optimization_barrier((message, weight))
        received = [message] + received
        later, message = call(
            functools.partial(group_kernel, steps, members, "net", stride, radix, len(inner)),
            (shape((rows, LANES), F32),) * 2,
            flops=20 * radix * rows * LANES,
            size=4 * radix * rows * LANES,
        )(*received, *inner)
        inner = (later,)
        stride *= radix
    radix = radices[-1]
    received = [message] + [
        exchange(message, "net", stride, radix, offset) for offset in range(1, radix)
    ]

    piece = shape((blocks // ranks, LANES), F32)
    incoming, *pieces = call(
        functools.partial(
            sums_kernel, steps, members, blocks, ranks, stride, radix, len(inner)
        ),
        (shape((steps * members, LANES), F32),) + (piece,) * ranks,
        scratch=[pltpu.VMEM((blocks, LANES), F32)],
        flops=20 * work,
        size=4 * work,
    )(
        *received, *inner, slot, weight, own_part, factor,
        inlet_values, inlet_rows, arriving, inlets,
    )
    chunks = next(n for n in (4, 2, 1) if blocks % n == 0)
    grad_lateral = call(
        functools.partial(grad_kernel, steps, members, blocks, chunks),
        shape((steps, members, reaches), jnp.bfloat16),
        scratch=[
            pltpu.VMEM((steps, members, reaches), jnp.bfloat16),
            pltpu.VMEM((blocks, LANES), F32),
            pltpu.SemaphoreType.DMA((chunks,)),
        ],
        flops=30 * work,
        size=6 * work,
        out_specs=pl.BlockSpec(memory_space=pl.ANY),
    )(incoming, own, response, slot, rough, factor)
    total = pieces[0]
    for offset in range(1, ranks):
        back = offset if is_power(ranks) else ranks - offset
        total = total + exchange(pieces[offset], "mem", 1, ranks, back)
    return grad_lateral, total.reshape(-1)


def solution(mesh):
    in_specs = (
        P(None, "mem", "net"),
        P(None, "mem", "net"),
        P(None, "mem", "net"),
        P("net"),
        P("net"),
        P("net", None, None),
        P("net"),
        P("net"),
        P("net", None),
    )
    out_specs = (P(None, "mem", "net"), P(("net", "mem")))
    return jax.shard_map(gradients, mesh=mesh, in_specs=in_specs, out_specs=out_specs, check_vma=False)
```

```python
import functools

import jax
import jax.numpy as jnp
from jax import lax
from jax.experimental import pallas as pl
from jax.experimental.pallas import tpu as pltpu
from jax.sharding import PartitionSpec as P


skew_weight = 0.2
LANES = 128
EXTRA = 8
F32 = jnp.float32


ROW_GATHER = lax.GatherDimensionNumbers(
    offset_dims=(), collapsed_slice_dims=(1,), start_index_map=(1,),
    operand_batching_dims=(0,), start_indices_batching_dims=(0,),
)
VMEM_BYTES = 20 << 20
GROUP = 8


def take(values, index):
    return lax.gather(
        values, index[..., None], ROW_GATHER, (1, 1),
        mode=lax.GatherScatterMode.PROMISE_IN_BOUNDS,
    )


def weights_of(travel):
    divisor = travel * (1.0 - skew_weight) + 0.5
    weight_new = (0.5 - travel * skew_weight) / divisor
    weight_old = (0.5 + travel * skew_weight) / divisor
    weight_stay = (travel * (1.0 - skew_weight) - 0.5) / divisor
    return weight_new, weight_old, weight_stay


def slopes_of(travel):
    divisor = travel * (1.0 - skew_weight) + 0.5
    square = divisor * divisor
    return (
        -0.5 / square,
        (skew_weight - 0.5) / square,
        (1.0 - skew_weight) / square,
        (skew_weight - 1.0) / square,
    )


def levels_of(lanes):
    count = 0
    while (1 << count) < lanes:
        count += 1
    return count


def split(value):
    high = value.astype(jnp.bfloat16)
    return high, (value - high.astype(F32)).astype(jnp.bfloat16)


def multiply_series(steps, left, right):
    result = []
    for lag in range(steps):
        total = left[0] * right[lag]
        for first in range(1, lag + 1):
            total = total + left[first] * right[lag - first]
        result.append(total)
    return result


def local_kernel(
    steps, members, blocks,
    flow_hbm, lateral_hbm, cot_hbm, matrix_hbm,
    rough_hbm, factor_hbm, down_hbm, exit_hbm, inlet_hbm,
    own_ref, message_ref, leaving_ref, response_ref, slot_ref, inlet_values_ref, inlet_rows_ref,
    flow_ref, lateral_ref, rough_ref, factor_ref, down_ref, inlet_ref,
    exit_ref, cot_ref, matrix_ref, stay_ref, ratio_ref,
    small_sem, cot_sem, matrix_sem, flow_sem, lateral_sem,
):
    small = [
        pltpu.make_async_copy(source, target, small_sem.at[i])
        for i, (source, target) in enumerate((
            (rough_hbm, rough_ref), (factor_hbm, factor_ref), (down_hbm, down_ref),
            (exit_hbm, exit_ref), (inlet_hbm, inlet_ref),
        ))
    ]
    large = []
    for i, first in enumerate(range(0, blocks, GROUP)):
        size = min(GROUP, blocks - first)
        lanes = pl.ds(first * LANES, size * LANES)
        part = pl.ds(first, size)
        large.append((
            pltpu.make_async_copy(matrix_hbm.at[part], matrix_ref.at[part], matrix_sem.at[i]),
            pltpu.make_async_copy(cot_hbm.at[:, :, lanes], cot_ref.at[:, :, lanes], cot_sem.at[i]),
            pltpu.make_async_copy(
                flow_hbm.at[:, :, lanes], flow_ref.at[:, :, lanes], flow_sem.at[i]
            ),
        ))
    lateral_copy = pltpu.make_async_copy(lateral_hbm, lateral_ref, lateral_sem)
    for copy in small:
        copy.start()
    for copies in large:
        for copy in copies:
            copy.start()
    lateral_copy.start()
    for copy in small:
        copy.wait()

    travel = rough_ref[...] * factor_ref[...]
    weight_new, weight_old, weight_stay = weights_of(travel)
    down = down_ref[...]
    lane = lax.broadcasted_iota(jnp.int32, down.shape, 1)
    interior = down < LANES
    pointer = jnp.where(interior, down, lane)
    next_new = take(weight_new, pointer)
    next_old = take(weight_old, pointer)
    ratio = jnp.where(interior, next_old / next_new, 0.0)
    stay_ref[...] = weight_stay
    ratio_ref[...] = ratio

    inlet = inlet_ref[...]
    inlet_block = inlet // LANES
    inlet_lane = inlet - inlet_block * LANES
    member_lane = jnp.broadcast_to(inlet_lane, (members, LANES))
    member_block = jnp.broadcast_to(inlet_block, (members, LANES))
    at_inlet = [jnp.zeros((members, LANES), F32)] * steps

    def solve_group(first, at_inlet):
        places = range(first, min(first + GROUP, blocks))
        tables = {
            block: jnp.concatenate(split(matrix_ref[block]), axis=1) for block in places
        }
        right, value = {}, {}
        for step in reversed(range(steps)):
            for block in places:
                lanes = pl.ds(block * LANES, LANES)
                row = pl.ds(block, 1)
                source = cot_ref[step, :, lanes]
                if step == steps - 1:
                    right[block] = source.astype(F32)
                    product = jnp.dot(source, tables[block], preferred_element_type=F32)
                    value[block] = product[:, :LANES] + product[:, LANES:]
                else:
                    right[block] = (
                        source.astype(F32)
                        + stay_ref[row, :] * value[block]
                        + ratio_ref[row, :] * (value[block] - right[block])
                    )
                    product = jnp.dot(
                        jnp.concatenate(split(right[block]), axis=0), tables[block],
                        preferred_element_type=F32,
                    )
                    value[block] = product[:members, :LANES] + (
                        product[members:, :LANES] + product[:members, LANES:]
                    )
                own_ref[step, :, lanes] = value[block]
                at_inlet[step] = jnp.where(
                    member_block == block, take(value[block], member_lane), at_inlet[step]
                )
        return at_inlet

    unit = jnp.where(exit_ref[...] >= 0, 1.0, 0.0).astype(F32)
    response = [unit]
    gain = [jnp.where(interior, next_new, 0.0)]
    base = jnp.where(interior, next_new * weight_stay + next_old, 0.0)
    for _ in range(1, steps):
        response.append(response[-1] * weight_stay)
        gain.append(base)
        base = base * weight_stay
    for level in range(levels_of(LANES)):
        pulled = [take(value, pointer) for value in response]
        added = multiply_series(steps, gain, pulled)
        response = [value + more for value, more in zip(response, added)]
        if level + 1 < levels_of(LANES):
            gain = multiply_series(steps, gain, [take(value, pointer) for value in gain])
        pointer = take(pointer, pointer)
    slot = take(exit_ref[...], pointer)
    slot = jnp.maximum(slot, 0)
    slot_ref[...] = slot
    for lag in range(steps):
        response_ref[lag] = response[lag]

    lane_rows = jnp.broadcast_to(inlet_lane, (blocks, LANES))
    block_rows = lax.broadcasted_iota(jnp.int32, (blocks, LANES), 0)
    chosen = block_rows == jnp.broadcast_to(inlet_block, (blocks, LANES))

    def at_inlets(rows):
        return jnp.sum(jnp.where(chosen, take(rows, lane_rows), 0.0), axis=0, keepdims=True)

    travel_in = at_inlets(travel)
    slot_in = at_inlets(slot.astype(F32))
    response_in = [at_inlets(value) for value in response]
    new_in, old_in, _ = weights_of(travel_in)

    sub = lax.broadcasted_iota(jnp.int32, (LANES, LANES), 0)
    leaving = None
    for turn, first in enumerate(range(0, blocks, GROUP)):
        for copy in large[turn]:
            copy.wait()
        at_inlet = solve_group(first, list(at_inlet))
        for block in range(first, min(first + GROUP, blocks)):
            lanes = pl.ds(block * LANES, LANES)
            table = (sub == exit_ref[pl.ds(block, 1), :]).astype(F32).astype(jnp.bfloat16)
            part = lax.dot_general(
                flow_ref[:, :, lanes].reshape((steps + 1) * members, LANES), table,
                (((1,), (1,)), ((), ())), preferred_element_type=F32,
            )
            leaving = part if leaving is None else leaving + part
    leaving_ref[...] = leaving

    for step in range(steps):
        rows = pl.ds(step * members, members)
        inlet_values_ref[rows, :] = at_inlet[step]
        outgoing = new_in * at_inlet[step]
        if step + 1 < steps:
            outgoing = outgoing + old_in * at_inlet[step + 1]
        message_ref[rows, :] = outgoing
    tail = []
    for lag in range(steps):
        coefficient = new_in * response_in[lag]
        if lag > 0:
            coefficient = coefficient + old_in * response_in[lag - 1]
        tail.append(coefficient)
    message_ref[pl.ds(steps * members, EXTRA), :] = eight_rows(tail + [slot_in])
    inlet_rows_ref[...] = eight_rows(response_in + [travel_in, slot_in])
    lateral_copy.wait()


def eight_rows(rows):
    rows = list(rows)
    while len(rows) % EXTRA:
        rows.append(jnp.zeros_like(rows[0]))
    return jnp.concatenate(rows, axis=0)


def compose(steps, members, upper, lower):
    values, coefficients, slot = upper
    below, below_coefficients, below_slot = lower
    index = jnp.broadcast_to(slot, (members, LANES)).astype(jnp.int32)
    pulled = [take(value, index) for value in below]
    result = []
    for step in range(steps):
        total = values[step]
        for lag in range(steps - step):
            total = total + coefficients[lag] * pulled[step + lag]
        result.append(total)
    if below_coefficients is None:
        return result, None, None
    table = eight_rows(list(below_coefficients) + [below_slot])
    table = take(table, jnp.broadcast_to(slot, table.shape).astype(jnp.int32))
    combined = multiply_series(
        steps, coefficients, [table[lag:lag + 1] for lag in range(steps)]
    )
    return result, combined, table[steps:steps + 1]


def read_message(steps, members, ref):
    values = [ref[pl.ds(step * members, members), :] for step in range(steps)]
    tail = ref[pl.ds(steps * members, EXTRA), :]
    return values, [tail[lag:lag + 1] for lag in range(steps)], tail[steps:steps + 1]


def write_message(steps, members, ref, message):
    values, coefficients, slot = message
    for step in range(steps):
        ref[pl.ds(step * members, members), :] = values[step]
    ref[pl.ds(steps * members, EXTRA), :] = eight_rows(list(coefficients) + [slot])


def identity_message(steps, members):
    zero = jnp.zeros((members, LANES), F32)
    row = jnp.zeros((1, LANES), F32)
    lane = lax.broadcasted_iota(jnp.int32, (8, LANES), 1).astype(F32)[0:1]
    return [zero] * steps, [row + 1.0] + [row] * (steps - 1), lane


def digit_of(axis, stride, radix):
    return (lax.axis_index(axis) // stride) % radix


def group_kernel(steps, members, axis, stride, radix, has_inner, *refs):
    messages = refs[:radix]
    inner = refs[radix] if has_inner else None
    outs = refs[radix + has_inner:]
    digit = digit_of(axis, stride, radix)
    for mine in range(radix):
        @pl.when(digit == mine)
        def _(mine=mine):
            total = None
            later = None
            for other in reversed(range(radix)):
                message = read_message(steps, members, messages[source_of(mine, other, radix)])
                total = message if total is None else compose(steps, members, message, total)
                if other == mine + 1:
                    later = total
            if later is None:
                later = identity_message(steps, members)
            if has_inner:
                later = compose(steps, members, read_message(steps, members, inner), later)
            write_message(steps, members, outs[0], later)
            write_message(steps, members, outs[1], total)


def last_round(steps, members, axis, stride, radix, messages, inner, out):
    digit = digit_of(axis, stride, radix)
    for mine in range(radix):
        @pl.when(digit == mine)
        def _(mine=mine):
            value = [jnp.zeros((members, LANES), F32)] * steps
            for other in reversed(range(mine + 1, radix)):
                message = read_message(steps, members, messages[source_of(mine, other, radix)])
                if other == radix - 1:
                    value = message[0]
                else:
                    value = compose(steps, members, message, (value, None, None))[0]
            if inner is not None:
                within = read_message(steps, members, inner)
                if mine == radix - 1:
                    value = within[0]
                else:
                    value = compose(steps, members, within, (value, None, None))[0]
            for step in range(steps):
                out[pl.ds(step * members, members), :] = value[step]


def is_power(number):
    return number & (number - 1) == 0


def source_of(mine, other, radix):
    return mine ^ other if is_power(radix) else (other - mine) % radix


def exchange(value, axis, stride, radix, offset):
    pairs = []
    for device in range(lax.axis_size(axis)):
        digit = (device // stride) % radix
        source = digit ^ offset if is_power(radix) else (digit + offset) % radix
        pairs.append((device + (source - digit) * stride, device))
    return lax.ppermute(value, axis, pairs)


def radices_of(count):
    radices = []
    while count > 1:
        radix = next(r for r in (4, 2, 3, 5, 7, count) if count % r == 0)
        radices.append(radix)
        count //= radix
    return radices or [1]


def weight_kernel(
    steps, members, blocks,
    flow_ref, lateral_ref, own_ref, response_ref, rough_ref, factor_ref, down_ref,
    weight_ref, part_ref, slopes_ref,
):
    slopes = slopes_of(rough_ref[...] * factor_ref[...])
    for i in range(4):
        slopes_ref[i] = slopes[i]
    sub = lax.broadcasted_iota(jnp.int32, (LANES, LANES), 0)

    def one_block(block, carry):
        lanes = pl.ds(pl.multiple_of(block * LANES, LANES), LANES)
        row = pl.ds(block, 1)
        table = (sub == down_ref[row, :]).astype(F32).astype(jnp.bfloat16)
        flows = flow_ref[:, :, lanes].reshape((steps + 1) * members, LANES)
        inflow = lax.dot_general(
            flows, table, (((1,), (1,)), ((), ())), preferred_element_type=F32
        )
        new, old, stay, side = (slopes_ref[i, row, :] for i in range(4))
        total = jnp.zeros((members, LANES), F32)
        weights = []
        for step in range(steps):
            now = inflow[(step + 1) * members:(step + 2) * members]
            prior = inflow[step * members:(step + 1) * members]
            weight = (
                new * now
                + old * prior
                + stay * flow_ref[step, :, lanes].astype(F32)
                + side * lateral_ref[step, :, lanes].astype(F32)
            )
            weights.append(weight)
            total = total + weight * own_ref[step, :, lanes]
            folded = response_ref[0, row, :] * weight
            for lag in range(1, step + 1):
                folded = folded + response_ref[lag, row, :] * weights[step - lag]
            weight_ref[step, :, lanes] = folded
        part_ref[row, :] = jnp.sum(total, axis=0, keepdims=True)
        return carry

    lax.fori_loop(0, blocks, one_block, 0, unroll=8)


def sums_kernel(steps, members, blocks, ranks, stride, radix, has_inner, *refs):
    messages, refs = refs[:radix], refs[radix:]
    inner, refs = (refs[0], refs[1:]) if has_inner else (None, refs)
    (
        slot_ref, weight_ref, own_part_ref, factor_ref,
        inlet_values_ref, inlet_rows_ref, arriving_ref, inlet_ref,
    ) = refs[:8]
    incoming_ref = refs[8]
    pieces = refs[9:9 + ranks]
    (part_ref,) = refs[9 + ranks:]
    last_round(steps, members, "net", stride, radix, messages, inner, incoming_ref)
    shape = (members, LANES)

    def one_block(block, carry):
        lanes = pl.ds(pl.multiple_of(block * LANES, LANES), LANES)
        row = pl.ds(block, 1)
        index = jnp.broadcast_to(slot_ref[row, :], shape)
        pulled = [
            take(incoming_ref[pl.ds(step * members, members), :], index) for step in range(steps)
        ]
        total = pulled[0] * weight_ref[0, :, lanes]
        for step in range(1, steps):
            total = total + pulled[step] * weight_ref[step, :, lanes]
        part_ref[row, :] = own_part_ref[row, :] + jnp.sum(total, axis=0, keepdims=True)
        return carry

    lax.fori_loop(0, blocks, one_block, 0, unroll=16)

    rows = inlet_rows_ref[...]
    slope_new, slope_old, _, _ = slopes_of(rows[steps:steps + 1])
    index = jnp.broadcast_to(rows[steps + 1:steps + 2], shape).astype(jnp.int32)
    pulled = [
        take(incoming_ref[pl.ds(step * members, members), :], index) for step in range(steps)
    ]
    total = jnp.zeros(shape, F32)
    for step in range(steps):
        value = inlet_values_ref[pl.ds(step * members, members), :]
        for lag in range(steps - step):
            value = value + rows[lag:lag + 1] * pulled[step + lag]
        total = total + value * (
            slope_new * arriving_ref[pl.ds((step + 1) * members, members), :]
            + slope_old * arriving_ref[pl.ds(step * members, members), :]
        )
    at_inlet = jnp.sum(total, axis=0, keepdims=True)
    inlet = inlet_ref[...]
    inlet_block = inlet // LANES
    inlet_lane = inlet - inlet_block * LANES
    block_rows = lax.broadcasted_iota(jnp.int32, (blocks, LANES), 0)
    spread = jnp.where(block_rows == inlet_block, at_inlet, 0.0)
    lane_table = (
        lax.broadcasted_iota(jnp.int32, (LANES, LANES), 0)
        == jnp.broadcast_to(inlet_lane, (LANES, LANES))
    ).astype(F32)
    placed = lax.dot_general(
        spread, lane_table, (((1,), (1,)), ((), ())),
        precision=lax.Precision.HIGHEST, preferred_element_type=F32,
    )
    part_ref[...] = factor_ref[...] * (part_ref[...] + placed)
    mine = lax.axis_index("mem")
    piece = blocks // ranks
    for offset in range(ranks):
        target = mine ^ offset if is_power(ranks) else (mine + offset) % ranks
        pieces[offset][...] = part_ref[pl.ds(pl.multiple_of(target * piece, piece), piece), :]


def grad_kernel(
    steps, members, blocks, chunks,
    incoming_ref, own_ref, response_ref, slot_ref, rough_ref, factor_ref,
    grad_hbm, grad_ref, side_ref, sem,
):
    side_ref[...] = 1.0 / (rough_ref[...] * factor_ref[...] * (1.0 - skew_weight) + 0.5)
    shape = (members, LANES)
    part = blocks // chunks

    def one_block(block, carry):
        lanes = pl.ds(pl.multiple_of(block * LANES, LANES), LANES)
        row = pl.ds(block, 1)
        index = jnp.broadcast_to(slot_ref[row, :], shape)
        pulled = [
            take(incoming_ref[pl.ds(step * members, members), :], index) for step in range(steps)
        ]
        for step in range(steps):
            value = own_ref[step, :, lanes]
            for lag in range(steps - step):
                value = value + response_ref[lag, row, :] * pulled[step + lag]
            grad_ref[step, :, lanes] = (side_ref[row, :] * value).astype(jnp.bfloat16)
        return carry

    copies = []
    for chunk in range(chunks):
        lax.fori_loop(chunk * part, (chunk + 1) * part, one_block, 0, unroll=8)
        lanes = pl.ds(chunk * part * LANES, part * LANES)
        copies.append(pltpu.make_async_copy(
            grad_ref.at[:, :, lanes], grad_hbm.at[:, :, lanes], sem.at[chunk]
        ))
        copies[-1].start()
    for copy in copies:
        copy.wait()


def call(kernel, out_shape, scratch=(), flops=0, size=0, **specs):
    return pl.pallas_call(
        kernel,
        out_shape=out_shape,
        **specs,
        scratch_shapes=scratch,
        compiler_params=pltpu.CompilerParams(vmem_limit_bytes=VMEM_BYTES),
        cost_estimate=pl.CostEstimate(flops=flops, bytes_accessed=size, transcendentals=0),
    )


def gradients(
    stored_reach_flows, lateral, cotangent, roughness, travel_factor,
    inverse_block_matrix, down_in_block, exit_slot, inlet_reach,
):
    steps, members, reaches = cotangent.shape
    blocks = reaches // LANES
    count = lax.axis_size("net")
    ranks = lax.axis_size("mem")
    rough = roughness.reshape(blocks, LANES)
    factor = travel_factor.reshape(blocks, LANES)
    down = down_in_block.reshape(blocks, LANES)
    leave = exit_slot.reshape(blocks, LANES)
    rows = steps * members + EXTRA
    shape = jax.ShapeDtypeStruct
    work = steps * members * reaches

    hbm = pl.BlockSpec(memory_space=pltpu.HBM)

    def stay_out(array):
        return pltpu.with_memory_space_constraint(array, pltpu.HBM)

    small = (rough, factor, down, leave, inlet_reach)
    turns = -(-blocks // GROUP)
    (
        own, message, leaving, response, slot, inlet_values, inlet_rows,
        flows, lateral, rough, factor, down, inlets,
    ) = call(
        functools.partial(local_kernel, steps, members, blocks),
        (
            shape((steps, members, reaches), F32),
            shape((rows, LANES), F32),
            shape(((steps + 1) * members, LANES), F32),
            shape((steps, blocks, LANES), F32),
            shape((blocks, LANES), jnp.int32),
            shape((steps * members, LANES), F32),
            shape((EXTRA, LANES), F32),
        ) + tuple(
            shape(array.shape, array.dtype)
            for array in (stored_reach_flows, lateral, rough, factor, down, inlet_reach)
        ),
        scratch=[
            pltpu.VMEM(leave.shape, leave.dtype),
            pltpu.VMEM(cotangent.shape, cotangent.dtype),
            pltpu.VMEM(inverse_block_matrix.shape, inverse_block_matrix.dtype),
            pltpu.VMEM((blocks, LANES), F32),
            pltpu.VMEM((blocks, LANES), F32),
            pltpu.SemaphoreType.DMA((len(small),)),
            pltpu.SemaphoreType.DMA((turns,)),
            pltpu.SemaphoreType.DMA((turns,)),
            pltpu.SemaphoreType.DMA((turns,)),
            pltpu.SemaphoreType.DMA,
        ],
        flops=10 * LANES * work,
        size=10 * work,
        in_specs=[hbm] * (4 + len(small)),
    )(*(
        stay_out(array)
        for array in (stored_reach_flows, lateral, cotangent, inverse_block_matrix) + small
    ))

    weight, own_part = call(
        functools.partial(weight_kernel, steps, members, blocks),
        (shape((steps, members, reaches), F32), shape((blocks, LANES), F32)),
        scratch=[pltpu.VMEM((4, blocks, LANES), F32)],
        flops=2 * LANES * work,
        size=8 * work,
    )(flows, lateral, own, response, rough, factor, down)

    stride = 1
    inner = ()
    radices = radices_of(count)
    for turn, radix in enumerate(radices[:-1]):
        received = [message] + [
            exchange(message, "net", stride, radix, offset) for offset in range(1, radix)
        ]
        if turn == 0:
            arriving = lax.ppermute(leaving, "net", [(i, i + 1) for i in range(count - 1)])
        later, message = call(
            functools.partial(group_kernel, steps, members, "net", stride, radix, len(inner)),
            (shape((rows, LANES), F32),) * 2,
            flops=20 * radix * rows * LANES,
            size=4 * radix * rows * LANES,
        )(*received, *inner)
        inner = (later,)
        stride *= radix
    radix = radices[-1]
    if len(radices) == 1:
        arriving = lax.ppermute(leaving, "net", [(i, i + 1) for i in range(count - 1)])
    received = [message] + [
        exchange(message, "net", stride, radix, offset) for offset in range(1, radix)
    ]

    piece = shape((blocks // ranks, LANES), F32)
    incoming, *pieces = call(
        functools.partial(
            sums_kernel, steps, members, blocks, ranks, stride, radix, len(inner)
        ),
        (shape((steps * members, LANES), F32),) + (piece,) * ranks,
        scratch=[pltpu.VMEM((blocks, LANES), F32)],
        flops=20 * work,
        size=4 * work,
    )(
        *received, *inner, slot, weight, own_part, factor,
        inlet_values, inlet_rows, arriving, inlets,
    )
    chunks = next(n for n in (4, 2, 1) if blocks % n == 0)
    grad_lateral = call(
        functools.partial(grad_kernel, steps, members, blocks, chunks),
        shape((steps, members, reaches), jnp.bfloat16),
        scratch=[
            pltpu.VMEM((steps, members, reaches), jnp.bfloat16),
            pltpu.VMEM((blocks, LANES), F32),
            pltpu.SemaphoreType.DMA((chunks,)),
        ],
        flops=30 * work,
        size=6 * work,
        out_specs=pl.BlockSpec(memory_space=pl.ANY),
    )(incoming, own, response, slot, rough, factor)
    total = pieces[0]
    for offset in range(1, ranks):
        back = offset if is_power(ranks) else ranks - offset
        total = total + exchange(pieces[offset], "mem", 1, ranks, back)
    return grad_lateral, total.reshape(-1)


def solution(mesh):
    in_specs = (
        P(None, "mem", "net"),
        P(None, "mem", "net"),
        P(None, "mem", "net"),
        P("net"),
        P("net"),
        P("net", None, None),
        P("net"),
        P("net"),
        P("net", None),
    )
    out_specs = (P(None, "mem", "net"), P(("net", "mem")))
    return jax.shard_map(gradients, mesh=mesh, in_specs=in_specs, out_specs=out_specs, check_vma=False)
```

```python
import functools

import jax
import jax.numpy as jnp
from jax import lax
from jax.experimental import pallas as pl
from jax.experimental.pallas import tpu as pltpu
from jax.sharding import PartitionSpec as P


skew_weight = 0.2
LANES = 128
EXTRA = 8
F32 = jnp.float32


ROW_GATHER = lax.GatherDimensionNumbers(
    offset_dims=(), collapsed_slice_dims=(1,), start_index_map=(1,),
    operand_batching_dims=(0,), start_indices_batching_dims=(0,),
)
VMEM_BYTES = 20 << 20
GROUP = 16
CHUNK = 8


def take(values, index):
    return lax.gather(
        values, index[..., None], ROW_GATHER, (1, 1),
        mode=lax.GatherScatterMode.PROMISE_IN_BOUNDS,
    )


def weights_of(travel):
    divisor = travel * (1.0 - skew_weight) + 0.5
    weight_new = (0.5 - travel * skew_weight) / divisor
    weight_old = (0.5 + travel * skew_weight) / divisor
    weight_stay = (travel * (1.0 - skew_weight) - 0.5) / divisor
    return weight_new, weight_old, weight_stay


def slopes_of(travel):
    divisor = travel * (1.0 - skew_weight) + 0.5
    square = divisor * divisor
    return (
        -0.5 / square,
        (skew_weight - 0.5) / square,
        (1.0 - skew_weight) / square,
        (skew_weight - 1.0) / square,
    )


def levels_of(lanes):
    count = 0
    while (1 << count) < lanes:
        count += 1
    return count


def split(value):
    high = value.astype(jnp.bfloat16)
    return high, (value - high.astype(F32)).astype(jnp.bfloat16)


def multiply_series(steps, left, right):
    result = []
    for lag in range(steps):
        total = left[0] * right[lag]
        for first in range(1, lag + 1):
            total = total + left[first] * right[lag - first]
        result.append(total)
    return result


def local_kernel(
    steps, members, blocks,
    cot_ref, matrix_ref, rough_ref, factor_ref, down_ref, exit_ref, inlet_ref, lateral_hbm,
    own_ref, message_ref, response_ref, slot_ref, inlet_values_ref, inlet_rows_ref, lateral_ref,
    stay_ref, ratio_ref, lateral_sem,
):
    lateral_copy = pltpu.make_async_copy(lateral_hbm, lateral_ref, lateral_sem)
    lateral_copy.start()

    travel = rough_ref[...] * factor_ref[...]
    weight_new, weight_old, weight_stay = weights_of(travel)
    down = down_ref[...]
    lane = lax.broadcasted_iota(jnp.int32, down.shape, 1)
    interior = down < LANES
    pointer = jnp.where(interior, down, lane)
    next_new = take(weight_new, pointer)
    next_old = take(weight_old, pointer)
    ratio = jnp.where(interior, next_old / next_new, 0.0)
    stay_ref[...] = weight_stay
    ratio_ref[...] = ratio

    inlet = inlet_ref[...]
    inlet_block = inlet // LANES
    inlet_lane = inlet - inlet_block * LANES
    member_lane = jnp.broadcast_to(inlet_lane, (members, LANES))
    member_block = jnp.broadcast_to(inlet_block, (members, LANES))
    at_inlet = [jnp.zeros((members, LANES), F32)] * steps

    def solve_group(first, at_inlet):
        places = range(first, min(first + GROUP, blocks))
        tables = {
            block: jnp.concatenate(split(matrix_ref[block]), axis=1) for block in places
        }
        right, value = {}, {}
        for step in reversed(range(steps)):
            for block in places:
                lanes = pl.ds(block * LANES, LANES)
                row = pl.ds(block, 1)
                source = cot_ref[step, :, lanes]
                if step == steps - 1:
                    right[block] = source.astype(F32)
                    product = jnp.dot(source, tables[block], preferred_element_type=F32)
                    value[block] = product[:, :LANES] + product[:, LANES:]
                else:
                    right[block] = (
                        source.astype(F32)
                        + stay_ref[row, :] * value[block]
                        + ratio_ref[row, :] * (value[block] - right[block])
                    )
                    product = jnp.dot(
                        jnp.concatenate(split(right[block]), axis=0), tables[block],
                        preferred_element_type=F32,
                    )
                    value[block] = product[:members, :LANES] + (
                        product[members:, :LANES] + product[:members, LANES:]
                    )
                own_ref[step, :, lanes] = value[block]
                at_inlet[step] = jnp.where(
                    member_block == block, take(value[block], member_lane), at_inlet[step]
                )
        return at_inlet

    unit = jnp.where(exit_ref[...] >= 0, 1.0, 0.0).astype(F32)
    response = [unit]
    gain = [jnp.where(interior, next_new, 0.0)]
    base = jnp.where(interior, next_new * weight_stay + next_old, 0.0)
    for _ in range(1, steps):
        response.append(response[-1] * weight_stay)
        gain.append(base)
        base = base * weight_stay
    for level in range(levels_of(LANES)):
        pulled = [take(value, pointer) for value in response]
        added = multiply_series(steps, gain, pulled)
        response = [value + more for value, more in zip(response, added)]
        if level + 1 < levels_of(LANES):
            gain = multiply_series(steps, gain, [take(value, pointer) for value in gain])
        pointer = take(pointer, pointer)
    slot = take(exit_ref[...], pointer)
    slot = jnp.maximum(slot, 0)
    slot_ref[...] = slot
    for lag in range(steps):
        response_ref[lag] = response[lag]

    lane_rows = jnp.broadcast_to(inlet_lane, (blocks, LANES))
    block_rows = lax.broadcasted_iota(jnp.int32, (blocks, LANES), 0)
    chosen = block_rows == jnp.broadcast_to(inlet_block, (blocks, LANES))

    def at_inlets(rows):
        return jnp.sum(jnp.where(chosen, take(rows, lane_rows), 0.0), axis=0, keepdims=True)

    travel_in = at_inlets(travel)
    slot_in = at_inlets(slot.astype(F32))
    response_in = [at_inlets(value) for value in response]
    new_in, old_in, _ = weights_of(travel_in)

    for first in range(0, blocks, GROUP):
        at_inlet = solve_group(first, list(at_inlet))

    for step in range(steps):
        rows = pl.ds(step * members, members)
        inlet_values_ref[rows, :] = at_inlet[step]
        outgoing = new_in * at_inlet[step]
        if step + 1 < steps:
            outgoing = outgoing + old_in * at_inlet[step + 1]
        message_ref[rows, :] = outgoing
    tail = []
    for lag in range(steps):
        coefficient = new_in * response_in[lag]
        if lag > 0:
            coefficient = coefficient + old_in * response_in[lag - 1]
        tail.append(coefficient)
    message_ref[pl.ds(steps * members, EXTRA), :] = eight_rows(tail + [slot_in])
    inlet_rows_ref[...] = eight_rows(response_in + [travel_in, slot_in])
    lateral_copy.wait()


def fetch_kernel(steps, members, blocks, count, *refs):
    sources, targets = refs[:count], refs[count:2 * count]
    leaving_ref, flow_sem, sem = refs[2 * count:]
    flow_hbm, flow_ref = sources[0], targets[0]
    exit_ref = targets[1]
    flow_copies = []
    for turn, first in enumerate(range(0, blocks, CHUNK)):
        lanes = pl.ds(first * LANES, min(CHUNK, blocks - first) * LANES)
        flow_copies.append(pltpu.make_async_copy(
            flow_hbm.at[:, :, lanes], flow_ref.at[:, :, lanes], flow_sem.at[turn]
        ))
    copies = [
        pltpu.make_async_copy(sources[i], targets[i], sem.at[i]) for i in range(1, count)
    ]
    copies[0].start()
    for copy in flow_copies:
        copy.start()
    for copy in copies[1:]:
        copy.start()
    copies[0].wait()
    sub = lax.broadcasted_iota(jnp.int32, (LANES, LANES), 0)
    total = None
    for block in range(blocks):
        if block % CHUNK == 0:
            flow_copies[block // CHUNK].wait()
        lanes = pl.ds(block * LANES, LANES)
        table = (sub == exit_ref[pl.ds(block, 1), :]).astype(F32).astype(jnp.bfloat16)
        flows = flow_ref[:, :, lanes].reshape((steps + 1) * members, LANES)
        part = lax.dot_general(
            flows, table, (((1,), (1,)), ((), ())), preferred_element_type=F32
        )
        total = part if total is None else total + part
    leaving_ref[...] = total
    for copy in copies[1:]:
        copy.wait()


def eight_rows(rows):
    rows = list(rows)
    while len(rows) % EXTRA:
        rows.append(jnp.zeros_like(rows[0]))
    return jnp.concatenate(rows, axis=0)


def compose(steps, members, upper, lower):
    values, coefficients, slot = upper
    below, below_coefficients, below_slot = lower
    index = jnp.broadcast_to(slot, (members, LANES)).astype(jnp.int32)
    pulled = [take(value, index) for value in below]
    result = []
    for step in range(steps):
        total = values[step]
        for lag in range(steps - step):
            total = total + coefficients[lag] * pulled[step + lag]
        result.append(total)
    if below_coefficients is None:
        return result, None, None
    table = eight_rows(list(below_coefficients) + [below_slot])
    table = take(table, jnp.broadcast_to(slot, table.shape).astype(jnp.int32))
    combined = multiply_series(
        steps, coefficients, [table[lag:lag + 1] for lag in range(steps)]
    )
    return result, combined, table[steps:steps + 1]


def read_message(steps, members, ref):
    values = [ref[pl.ds(step * members, members), :] for step in range(steps)]
    tail = ref[pl.ds(steps * members, EXTRA), :]
    return values, [tail[lag:lag + 1] for lag in range(steps)], tail[steps:steps + 1]


def write_message(steps, members, ref, message):
    values, coefficients, slot = message
    for step in range(steps):
        ref[pl.ds(step * members, members), :] = values[step]
    ref[pl.ds(steps * members, EXTRA), :] = eight_rows(list(coefficients) + [slot])


def identity_message(steps, members):
    zero = jnp.zeros((members, LANES), F32)
    row = jnp.zeros((1, LANES), F32)
    lane = lax.broadcasted_iota(jnp.int32, (8, LANES), 1).astype(F32)[0:1]
    return [zero] * steps, [row + 1.0] + [row] * (steps - 1), lane


def digit_of(axis, stride, radix):
    return (lax.axis_index(axis) // stride) % radix


def group_kernel(steps, members, axis, stride, radix, has_inner, *refs):
    messages = refs[:radix]
    inner = refs[radix] if has_inner else None
    outs = refs[radix + has_inner:]
    digit = digit_of(axis, stride, radix)
    for mine in range(radix):
        @pl.when(digit == mine)
        def _(mine=mine):
            total = None
            later = None
            for other in reversed(range(radix)):
                message = read_message(steps, members, messages[source_of(mine, other, radix)])
                total = message if total is None else compose(steps, members, message, total)
                if other == mine + 1:
                    later = total
            if later is None:
                later = identity_message(steps, members)
            if has_inner:
                later = compose(steps, members, read_message(steps, members, inner), later)
            write_message(steps, members, outs[0], later)
            write_message(steps, members, outs[1], total)


def last_round(steps, members, axis, stride, radix, messages, inner, out):
    digit = digit_of(axis, stride, radix)
    for mine in range(radix):
        @pl.when(digit == mine)
        def _(mine=mine):
            value = [jnp.zeros((members, LANES), F32)] * steps
            for other in reversed(range(mine + 1, radix)):
                message = read_message(steps, members, messages[source_of(mine, other, radix)])
                if other == radix - 1:
                    value = message[0]
                else:
                    value = compose(steps, members, message, (value, None, None))[0]
            if inner is not None:
                within = read_message(steps, members, inner)
                if mine == radix - 1:
                    value = within[0]
                else:
                    value = compose(steps, members, within, (value, None, None))[0]
            for step in range(steps):
                out[pl.ds(step * members, members), :] = value[step]


def is_power(number):
    return number & (number - 1) == 0


def source_of(mine, other, radix):
    return mine ^ other if is_power(radix) else (other - mine) % radix


def exchange(value, axis, stride, radix, offset):
    pairs = []
    for device in range(lax.axis_size(axis)):
        digit = (device // stride) % radix
        source = digit ^ offset if is_power(radix) else (digit + offset) % radix
        pairs.append((device + (source - digit) * stride, device))
    return lax.ppermute(value, axis, pairs)


def radices_of(count):
    radices = []
    while count > 1:
        radix = next(r for r in (4, 2, 3, 5, 7, count) if count % r == 0)
        radices.append(radix)
        count //= radix
    return radices or [1]


def weight_kernel(
    steps, members, blocks,
    flow_ref, lateral_ref, own_ref, response_ref, rough_ref, factor_ref, down_ref,
    weight_ref, part_ref, slopes_ref,
):
    slopes = slopes_of(rough_ref[...] * factor_ref[...])
    for i in range(4):
        slopes_ref[i] = slopes[i]
    sub = lax.broadcasted_iota(jnp.int32, (LANES, LANES), 0)

    def one_block(block, carry):
        lanes = pl.ds(pl.multiple_of(block * LANES, LANES), LANES)
        row = pl.ds(block, 1)
        table = (sub == down_ref[row, :]).astype(F32).astype(jnp.bfloat16)
        flows = flow_ref[:, :, lanes].reshape((steps + 1) * members, LANES)
        inflow = lax.dot_general(
            flows, table, (((1,), (1,)), ((), ())), preferred_element_type=F32
        )
        new, old, stay, side = (slopes_ref[i, row, :] for i in range(4))
        total = jnp.zeros((members, LANES), F32)
        weights = []
        for step in range(steps):
            now = inflow[(step + 1) * members:(step + 2) * members]
            prior = inflow[step * members:(step + 1) * members]
            weight = (
                new * now
                + old * prior
                + stay * flow_ref[step, :, lanes].astype(F32)
                + side * lateral_ref[step, :, lanes].astype(F32)
            )
            weights.append(weight)
            total = total + weight * own_ref[step, :, lanes]
            folded = response_ref[0, row, :] * weight
            for lag in range(1, step + 1):
                folded = folded + response_ref[lag, row, :] * weights[step - lag]
            weight_ref[step, :, lanes] = folded
        part_ref[row, :] = jnp.sum(total, axis=0, keepdims=True)
        return carry

    lax.fori_loop(0, blocks, one_block, 0, unroll=8)


def sums_kernel(steps, members, blocks, ranks, stride, radix, has_inner, *refs):
    messages, refs = refs[:radix], refs[radix:]
    inner, refs = (refs[0], refs[1:]) if has_inner else (None, refs)
    (
        slot_ref, weight_ref, own_part_ref, factor_ref,
        inlet_values_ref, inlet_rows_ref, arriving_ref, inlet_ref,
    ) = refs[:8]
    incoming_ref = refs[8]
    pieces = refs[9:9 + ranks]
    (part_ref,) = refs[9 + ranks:]
    last_round(steps, members, "net", stride, radix, messages, inner, incoming_ref)
    shape = (members, LANES)

    def one_block(block, carry):
        lanes = pl.ds(pl.multiple_of(block * LANES, LANES), LANES)
        row = pl.ds(block, 1)
        index = jnp.broadcast_to(slot_ref[row, :], shape)
        pulled = [
            take(incoming_ref[pl.ds(step * members, members), :], index) for step in range(steps)
        ]
        total = pulled[0] * weight_ref[0, :, lanes]
        for step in range(1, steps):
            total = total + pulled[step] * weight_ref[step, :, lanes]
        part_ref[row, :] = own_part_ref[row, :] + jnp.sum(total, axis=0, keepdims=True)
        return carry

    lax.fori_loop(0, blocks, one_block, 0, unroll=16)

    rows = inlet_rows_ref[...]
    slope_new, slope_old, _, _ = slopes_of(rows[steps:steps + 1])
    index = jnp.broadcast_to(rows[steps + 1:steps + 2], shape).astype(jnp.int32)
    pulled = [
        take(incoming_ref[pl.ds(step * members, members), :], index) for step in range(steps)
    ]
    total = jnp.zeros(shape, F32)
    for step in range(steps):
        value = inlet_values_ref[pl.ds(step * members, members), :]
        for lag in range(steps - step):
            value = value + rows[lag:lag + 1] * pulled[step + lag]
        total = total + value * (
            slope_new * arriving_ref[pl.ds((step + 1) * members, members), :]
            + slope_old * arriving_ref[pl.ds(step * members, members), :]
        )
    at_inlet = jnp.sum(total, axis=0, keepdims=True)
    inlet = inlet_ref[...]
    inlet_block = inlet // LANES
    inlet_lane = inlet - inlet_block * LANES
    block_rows = lax.broadcasted_iota(jnp.int32, (blocks, LANES), 0)
    spread = jnp.where(block_rows == inlet_block, at_inlet, 0.0)
    lane_table = (
        lax.broadcasted_iota(jnp.int32, (LANES, LANES), 0)
        == jnp.broadcast_to(inlet_lane, (LANES, LANES))
    ).astype(F32)
    placed = lax.dot_general(
        spread, lane_table, (((1,), (1,)), ((), ())),
        precision=lax.Precision.HIGHEST, preferred_element_type=F32,
    )
    part_ref[...] = factor_ref[...] * (part_ref[...] + placed)
    mine = lax.axis_index("mem")
    piece = blocks // ranks
    for offset in range(ranks):
        target = mine ^ offset if is_power(ranks) else (mine + offset) % ranks
        pieces[offset][...] = part_ref[pl.ds(pl.multiple_of(target * piece, piece), piece), :]


def grad_kernel(
    steps, members, blocks, chunks,
    incoming_ref, own_ref, response_ref, slot_ref, rough_ref, factor_ref,
    grad_hbm, grad_ref, side_ref, sem,
):
    side_ref[...] = 1.0 / (rough_ref[...] * factor_ref[...] * (1.0 - skew_weight) + 0.5)
    shape = (members, LANES)
    part = blocks // chunks

    def one_block(block, carry):
        lanes = pl.ds(pl.multiple_of(block * LANES, LANES), LANES)
        row = pl.ds(block, 1)
        index = jnp.broadcast_to(slot_ref[row, :], shape)
        pulled = [
            take(incoming_ref[pl.ds(step * members, members), :], index) for step in range(steps)
        ]
        for step in range(steps):
            value = own_ref[step, :, lanes]
            for lag in range(steps - step):
                value = value + response_ref[lag, row, :] * pulled[step + lag]
            grad_ref[step, :, lanes] = (side_ref[row, :] * value).astype(jnp.bfloat16)
        return carry

    copies = []
    for chunk in range(chunks):
        lax.fori_loop(chunk * part, (chunk + 1) * part, one_block, 0, unroll=8)
        lanes = pl.ds(chunk * part * LANES, part * LANES)
        copies.append(pltpu.make_async_copy(
            grad_ref.at[:, :, lanes], grad_hbm.at[:, :, lanes], sem.at[chunk]
        ))
        copies[-1].start()
    for copy in copies:
        copy.wait()


def call(kernel, out_shape, scratch=(), flops=0, size=0, **specs):
    return pl.pallas_call(
        kernel,
        out_shape=out_shape,
        **specs,
        scratch_shapes=scratch,
        compiler_params=pltpu.CompilerParams(vmem_limit_bytes=VMEM_BYTES),
        cost_estimate=pl.CostEstimate(flops=flops, bytes_accessed=size, transcendentals=0),
    )


def gradients(
    stored_reach_flows, lateral, cotangent, roughness, travel_factor,
    inverse_block_matrix, down_in_block, exit_slot, inlet_reach,
):
    steps, members, reaches = cotangent.shape
    blocks = reaches // LANES
    count = lax.axis_size("net")
    ranks = lax.axis_size("mem")
    rough = roughness.reshape(blocks, LANES)
    factor = travel_factor.reshape(blocks, LANES)
    down = down_in_block.reshape(blocks, LANES)
    leave = exit_slot.reshape(blocks, LANES)
    rows = steps * members + EXTRA
    shape = jax.ShapeDtypeStruct
    work = steps * members * reaches

    hbm = pl.BlockSpec(memory_space=pltpu.HBM)

    def stay_out(array):
        return pltpu.with_memory_space_constraint(array, pltpu.HBM)

    inputs = (
        stored_reach_flows, leave, rough, factor, down, inlet_reach, inverse_block_matrix, cotangent
    )
    flows, leave, rough, factor, down, inlets, matrix, cotangent, leaving = call(
        functools.partial(fetch_kernel, steps, members, blocks, len(inputs)),
        tuple(shape(array.shape, array.dtype) for array in inputs)
        + (shape(((steps + 1) * members, LANES), F32),),
        scratch=[
            pltpu.SemaphoreType.DMA((-(-blocks // CHUNK),)),
            pltpu.SemaphoreType.DMA((len(inputs),)),
        ],
        flops=2 * LANES * work,
        size=9 * work,
        in_specs=[hbm] * len(inputs),
    )(*(stay_out(array) for array in inputs))
    own, message, response, slot, inlet_values, inlet_rows, lateral = call(
        functools.partial(local_kernel, steps, members, blocks),
        (
            shape((steps, members, reaches), F32),
            shape((rows, LANES), F32),
            shape((steps, blocks, LANES), F32),
            shape((blocks, LANES), jnp.int32),
            shape((steps * members, LANES), F32),
            shape((EXTRA, LANES), F32),
            shape(lateral.shape, lateral.dtype),
        ),
        scratch=[pltpu.VMEM((blocks, LANES), F32)] * 2 + [pltpu.SemaphoreType.DMA],
        flops=8 * LANES * work,
        size=6 * work,
        in_specs=[pl.BlockSpec()] * 7 + [hbm],
    )(cotangent, matrix, rough, factor, down, leave, inlets, stay_out(lateral))

    weight, own_part = call(
        functools.partial(weight_kernel, steps, members, blocks),
        (shape((steps, members, reaches), F32), shape((blocks, LANES), F32)),
        scratch=[pltpu.VMEM((4, blocks, LANES), F32)],
        flops=2 * LANES * work,
        size=8 * work,
    )(flows, lateral, own, response, rough, factor, down)

    stride = 1
    inner = ()
    radices = radices_of(count)
    for turn, radix in enumerate(radices[:-1]):
        received = [message] + [
            exchange(message, "net", stride, radix, offset) for offset in range(1, radix)
        ]
        if turn == 0:
            arriving = lax.ppermute(leaving, "net", [(i, i + 1) for i in range(count - 1)])
        later, message = call(
            functools.partial(group_kernel, steps, members, "net", stride, radix, len(inner)),
            (shape((rows, LANES), F32),) * 2,
            flops=20 * radix * rows * LANES,
            size=4 * radix * rows * LANES,
        )(*received, *inner)
        inner = (later,)
        stride *= radix
    radix = radices[-1]
    if len(radices) == 1:
        arriving = lax.ppermute(leaving, "net", [(i, i + 1) for i in range(count - 1)])
    received = [message] + [
        exchange(message, "net", stride, radix, offset) for offset in range(1, radix)
    ]

    piece = shape((blocks // ranks, LANES), F32)
    incoming, *pieces = call(
        functools.partial(
            sums_kernel, steps, members, blocks, ranks, stride, radix, len(inner)
        ),
        (shape((steps * members, LANES), F32),) + (piece,) * ranks,
        scratch=[pltpu.VMEM((blocks, LANES), F32)],
        flops=20 * work,
        size=4 * work,
    )(
        *received, *inner, slot, weight, own_part, factor,
        inlet_values, inlet_rows, arriving, inlets,
    )
    chunks = next(n for n in (4, 2, 1) if blocks % n == 0)
    grad_lateral = call(
        functools.partial(grad_kernel, steps, members, blocks, chunks),
        shape((steps, members, reaches), jnp.bfloat16),
        scratch=[
            pltpu.VMEM((steps, members, reaches), jnp.bfloat16),
            pltpu.VMEM((blocks, LANES), F32),
            pltpu.SemaphoreType.DMA((chunks,)),
        ],
        flops=30 * work,
        size=6 * work,
        out_specs=pl.BlockSpec(memory_space=pl.ANY),
    )(incoming, own, response, slot, rough, factor)
    total = pieces[0]
    for offset in range(1, ranks):
        back = offset if is_power(ranks) else ranks - offset
        total = total + exchange(pieces[offset], "mem", 1, ranks, back)
    return grad_lateral, total.reshape(-1)


def solution(mesh):
    in_specs = (
        P(None, "mem", "net"),
        P(None, "mem", "net"),
        P(None, "mem", "net"),
        P("net"),
        P("net"),
        P("net", None, None),
        P("net"),
        P("net"),
        P("net", None),
    )
    out_specs = (P(None, "mem", "net"), P(("net", "mem")))
    return jax.shard_map(gradients, mesh=mesh, in_specs=in_specs, out_specs=out_specs, check_vma=False)
```

```python
import functools

import jax
import jax.numpy as jnp
from jax import lax
from jax.experimental import pallas as pl
from jax.experimental.pallas import tpu as pltpu
from jax.sharding import PartitionSpec as P


skew_weight = 0.2
LANES = 128
EXTRA = 8
F32 = jnp.float32


ROW_GATHER = lax.GatherDimensionNumbers(
    offset_dims=(), collapsed_slice_dims=(1,), start_index_map=(1,),
    operand_batching_dims=(0,), start_indices_batching_dims=(0,),
)
VMEM_BYTES = 20 << 20
GROUP = 16
CHUNK = 32


def take(values, index):
    return lax.gather(
        values, index[..., None], ROW_GATHER, (1, 1),
        mode=lax.GatherScatterMode.PROMISE_IN_BOUNDS,
    )


def weights_of(travel):
    divisor = travel * (1.0 - skew_weight) + 0.5
    weight_new = (0.5 - travel * skew_weight) / divisor
    weight_old = (0.5 + travel * skew_weight) / divisor
    weight_stay = (travel * (1.0 - skew_weight) - 0.5) / divisor
    return weight_new, weight_old, weight_stay


def slopes_of(travel):
    divisor = travel * (1.0 - skew_weight) + 0.5
    square = divisor * divisor
    return (
        -0.5 / square,
        (skew_weight - 0.5) / square,
        (1.0 - skew_weight) / square,
        (skew_weight - 1.0) / square,
    )


def levels_of(lanes):
    count = 0
    while (1 << count) < lanes:
        count += 1
    return count


def split(value):
    high = value.astype(jnp.bfloat16)
    return high, (value - high.astype(F32)).astype(jnp.bfloat16)


def multiply_series(steps, left, right):
    result = []
    for lag in range(steps):
        total = left[0] * right[lag]
        for first in range(1, lag + 1):
            total = total + left[first] * right[lag - first]
        result.append(total)
    return result


def local_kernel(
    steps, members, blocks,
    cot_ref, matrix_ref, rough_ref, factor_ref, down_ref, exit_ref, inlet_ref, lateral_hbm,
    own_ref, message_ref, response_ref, slot_ref, inlet_values_ref, inlet_rows_ref, lateral_ref,
    stay_ref, ratio_ref, lateral_sem,
):
    lateral_copy = pltpu.make_async_copy(lateral_hbm, lateral_ref, lateral_sem)
    lateral_copy.start()

    travel = rough_ref[...] * factor_ref[...]
    weight_new, weight_old, weight_stay = weights_of(travel)
    down = down_ref[...]
    lane = lax.broadcasted_iota(jnp.int32, down.shape, 1)
    interior = down < LANES
    pointer = jnp.where(interior, down, lane)
    next_new = take(weight_new, pointer)
    next_old = take(weight_old, pointer)
    ratio = jnp.where(interior, next_old / next_new, 0.0)
    stay_ref[...] = weight_stay
    ratio_ref[...] = ratio

    inlet = inlet_ref[...]
    inlet_block = inlet // LANES
    inlet_lane = inlet - inlet_block * LANES
    member_lane = jnp.broadcast_to(inlet_lane, (members, LANES))
    member_block = jnp.broadcast_to(inlet_block, (members, LANES))
    at_inlet = [jnp.zeros((members, LANES), F32)] * steps

    def solve_group(first, at_inlet):
        places = range(first, min(first + GROUP, blocks))
        tables = {
            block: jnp.concatenate(split(matrix_ref[block]), axis=1) for block in places
        }
        right, value = {}, {}
        for step in reversed(range(steps)):
            for block in places:
                lanes = pl.ds(block * LANES, LANES)
                row = pl.ds(block, 1)
                source = cot_ref[step, :, lanes]
                if step == steps - 1:
                    right[block] = source.astype(F32)
                    product = jnp.dot(source, tables[block], preferred_element_type=F32)
                    value[block] = product[:, :LANES] + product[:, LANES:]
                else:
                    right[block] = (
                        source.astype(F32)
                        + stay_ref[row, :] * value[block]
                        + ratio_ref[row, :] * (value[block] - right[block])
                    )
                    product = jnp.dot(
                        jnp.concatenate(split(right[block]), axis=0), tables[block],
                        preferred_element_type=F32,
                    )
                    value[block] = product[:members, :LANES] + (
                        product[members:, :LANES] + product[:members, LANES:]
                    )
                own_ref[step, :, lanes] = value[block]
                at_inlet[step] = jnp.where(
                    member_block == block, take(value[block], member_lane), at_inlet[step]
                )
        return at_inlet

    unit = jnp.where(exit_ref[...] >= 0, 1.0, 0.0).astype(F32)
    response = [unit]
    gain = [jnp.where(interior, next_new, 0.0)]
    base = jnp.where(interior, next_new * weight_stay + next_old, 0.0)
    for _ in range(1, steps):
        response.append(response[-1] * weight_stay)
        gain.append(base)
        base = base * weight_stay
    for level in range(levels_of(LANES)):
        pulled = [take(value, pointer) for value in response]
        added = multiply_series(steps, gain, pulled)
        response = [value + more for value, more in zip(response, added)]
        if level + 1 < levels_of(LANES):
            gain = multiply_series(steps, gain, [take(value, pointer) for value in gain])
        pointer = take(pointer, pointer)
    slot = take(exit_ref[...], pointer)
    slot = jnp.maximum(slot, 0)
    slot_ref[...] = slot
    for lag in range(steps):
        response_ref[lag] = response[lag]

    lane_rows = jnp.broadcast_to(inlet_lane, (blocks, LANES))
    block_rows = lax.broadcasted_iota(jnp.int32, (blocks, LANES), 0)
    chosen = block_rows == jnp.broadcast_to(inlet_block, (blocks, LANES))

    def at_inlets(rows):
        return jnp.sum(jnp.where(chosen, take(rows, lane_rows), 0.0), axis=0, keepdims=True)

    travel_in = at_inlets(travel)
    slot_in = at_inlets(slot.astype(F32))
    response_in = [at_inlets(value) for value in response]
    new_in, old_in, _ = weights_of(travel_in)

    for first in range(0, blocks, GROUP):
        at_inlet = solve_group(first, list(at_inlet))

    for step in range(steps):
        rows = pl.ds(step * members, members)
        inlet_values_ref[rows, :] = at_inlet[step]
        outgoing = new_in * at_inlet[step]
        if step + 1 < steps:
            outgoing = outgoing + old_in * at_inlet[step + 1]
        message_ref[rows, :] = outgoing
    tail = []
    for lag in range(steps):
        coefficient = new_in * response_in[lag]
        if lag > 0:
            coefficient = coefficient + old_in * response_in[lag - 1]
        tail.append(coefficient)
    message_ref[pl.ds(steps * members, EXTRA), :] = eight_rows(tail + [slot_in])
    inlet_rows_ref[...] = eight_rows(response_in + [travel_in, slot_in])
    lateral_copy.wait()


def fetch_kernel(steps, members, blocks, count, *refs):
    sources, targets = refs[:count], refs[count:2 * count]
    leaving_ref, flow_sem, sem = refs[2 * count:]
    flow_hbm, flow_ref = sources[0], targets[0]
    exit_ref = targets[1]
    flow_copies = []
    for turn, first in enumerate(range(0, blocks, CHUNK)):
        lanes = pl.ds(first * LANES, min(CHUNK, blocks - first) * LANES)
        flow_copies.append(pltpu.make_async_copy(
            flow_hbm.at[:, :, lanes], flow_ref.at[:, :, lanes], flow_sem.at[turn]
        ))
    copies = [
        pltpu.make_async_copy(sources[i], targets[i], sem.at[i]) for i in range(1, count)
    ]
    copies[0].start()
    for copy in flow_copies:
        copy.start()
    for copy in copies[1:]:
        copy.start()
    copies[0].wait()
    sub = lax.broadcasted_iota(jnp.int32, (LANES, LANES), 0)
    total = None
    for block in range(blocks):
        if block % CHUNK == 0:
            flow_copies[block // CHUNK].wait()
        lanes = pl.ds(block * LANES, LANES)
        table = (sub == exit_ref[pl.ds(block, 1), :]).astype(F32).astype(jnp.bfloat16)
        flows = flow_ref[:, :, lanes].reshape((steps + 1) * members, LANES)
        part = lax.dot_general(
            flows, table, (((1,), (1,)), ((), ())), preferred_element_type=F32
        )
        total = part if total is None else total + part
    leaving_ref[...] = total
    for copy in copies[1:]:
        copy.wait()


def eight_rows(rows):
    rows = list(rows)
    while len(rows) % EXTRA:
        rows.append(jnp.zeros_like(rows[0]))
    return jnp.concatenate(rows, axis=0)


def compose(steps, members, upper, lower):
    values, coefficients, slot = upper
    below, below_coefficients, below_slot = lower
    index = jnp.broadcast_to(slot, (members, LANES)).astype(jnp.int32)
    pulled = [take(value, index) for value in below]
    result = []
    for step in range(steps):
        total = values[step]
        for lag in range(steps - step):
            total = total + coefficients[lag] * pulled[step + lag]
        result.append(total)
    if below_coefficients is None:
        return result, None, None
    table = eight_rows(list(below_coefficients) + [below_slot])
    table = take(table, jnp.broadcast_to(slot, table.shape).astype(jnp.int32))
    combined = multiply_series(
        steps, coefficients, [table[lag:lag + 1] for lag in range(steps)]
    )
    return result, combined, table[steps:steps + 1]


def read_message(steps, members, ref):
    values = [ref[pl.ds(step * members, members), :] for step in range(steps)]
    tail = ref[pl.ds(steps * members, EXTRA), :]
    return values, [tail[lag:lag + 1] for lag in range(steps)], tail[steps:steps + 1]


def write_message(steps, members, ref, message):
    values, coefficients, slot = message
    for step in range(steps):
        ref[pl.ds(step * members, members), :] = values[step]
    ref[pl.ds(steps * members, EXTRA), :] = eight_rows(list(coefficients) + [slot])


def identity_message(steps, members):
    zero = jnp.zeros((members, LANES), F32)
    row = jnp.zeros((1, LANES), F32)
    lane = lax.broadcasted_iota(jnp.int32, (8, LANES), 1).astype(F32)[0:1]
    return [zero] * steps, [row + 1.0] + [row] * (steps - 1), lane


def digit_of(axis, stride, radix):
    return (lax.axis_index(axis) // stride) % radix


def group_kernel(steps, members, axis, stride, radix, has_inner, *refs):
    messages = refs[:radix]
    inner = refs[radix] if has_inner else None
    outs = refs[radix + has_inner:]
    digit = digit_of(axis, stride, radix)
    for mine in range(radix):
        @pl.when(digit == mine)
        def _(mine=mine):
            total = None
            later = None
            for other in reversed(range(radix)):
                message = read_message(steps, members, messages[source_of(mine, other, radix)])
                total = message if total is None else compose(steps, members, message, total)
                if other == mine + 1:
                    later = total
            if later is None:
                later = identity_message(steps, members)
            if has_inner:
                later = compose(steps, members, read_message(steps, members, inner), later)
            write_message(steps, members, outs[0], later)
            write_message(steps, members, outs[1], total)


def last_round(steps, members, axis, stride, radix, messages, inner, out):
    digit = digit_of(axis, stride, radix)
    for mine in range(radix):
        @pl.when(digit == mine)
        def _(mine=mine):
            value = [jnp.zeros((members, LANES), F32)] * steps
            for other in reversed(range(mine + 1, radix)):
                message = read_message(steps, members, messages[source_of(mine, other, radix)])
                if other == radix - 1:
                    value = message[0]
                else:
                    value = compose(steps, members, message, (value, None, None))[0]
            if inner is not None:
                within = read_message(steps, members, inner)
                if mine == radix - 1:
                    value = within[0]
                else:
                    value = compose(steps, members, within, (value, None, None))[0]
            for step in range(steps):
                out[pl.ds(step * members, members), :] = value[step]


def is_power(number):
    return number & (number - 1) == 0


def source_of(mine, other, radix):
    return mine ^ other if is_power(radix) else (other - mine) % radix


def exchange(value, axis, stride, radix, offset):
    pairs = []
    for device in range(lax.axis_size(axis)):
        digit = (device // stride) % radix
        source = digit ^ offset if is_power(radix) else (digit + offset) % radix
        pairs.append((device + (source - digit) * stride, device))
    return lax.ppermute(value, axis, pairs)


def radices_of(count):
    radices = []
    while count > 1:
        radix = next(r for r in (4, 2, 3, 5, 7, count) if count % r == 0)
        radices.append(radix)
        count //= radix
    return radices or [1]


def weight_kernel(
    steps, members, blocks,
    flow_ref, lateral_ref, own_ref, response_ref, rough_ref, factor_ref, down_ref,
    weight_ref, part_ref, slopes_ref,
):
    slopes = slopes_of(rough_ref[...] * factor_ref[...])
    for i in range(4):
        slopes_ref[i] = slopes[i]
    sub = lax.broadcasted_iota(jnp.int32, (LANES, LANES), 0)

    def one_block(block, carry):
        lanes = pl.ds(pl.multiple_of(block * LANES, LANES), LANES)
        row = pl.ds(block, 1)
        table = (sub == down_ref[row, :]).astype(F32).astype(jnp.bfloat16)
        flows = flow_ref[:, :, lanes].reshape((steps + 1) * members, LANES)
        inflow = lax.dot_general(
            flows, table, (((1,), (1,)), ((), ())), preferred_element_type=F32
        )
        new, old, stay, side = (slopes_ref[i, row, :] for i in range(4))
        total = jnp.zeros((members, LANES), F32)
        weights = []
        for step in range(steps):
            now = inflow[(step + 1) * members:(step + 2) * members]
            prior = inflow[step * members:(step + 1) * members]
            weight = (
                new * now
                + old * prior
                + stay * flow_ref[step, :, lanes].astype(F32)
                + side * lateral_ref[step, :, lanes].astype(F32)
            )
            weights.append(weight)
            total = total + weight * own_ref[step, :, lanes]
            folded = response_ref[0, row, :] * weight
            for lag in range(1, step + 1):
                folded = folded + response_ref[lag, row, :] * weights[step - lag]
            weight_ref[step, :, lanes] = folded
        part_ref[row, :] = jnp.sum(total, axis=0, keepdims=True)
        return carry

    lax.fori_loop(0, blocks, one_block, 0, unroll=8)


def sums_kernel(steps, members, blocks, ranks, stride, radix, has_inner, *refs):
    messages, refs = refs[:radix], refs[radix:]
    inner, refs = (refs[0], refs[1:]) if has_inner else (None, refs)
    (
        slot_ref, weight_ref, own_part_ref, factor_ref,
        inlet_values_ref, inlet_rows_ref, arriving_ref, inlet_ref,
    ) = refs[:8]
    incoming_ref = refs[8]
    pieces = refs[9:9 + ranks]
    (part_ref,) = refs[9 + ranks:]
    last_round(steps, members, "net", stride, radix, messages, inner, incoming_ref)
    shape = (members, LANES)

    def one_block(block, carry):
        lanes = pl.ds(pl.multiple_of(block * LANES, LANES), LANES)
        row = pl.ds(block, 1)
        index = jnp.broadcast_to(slot_ref[row, :], shape)
        pulled = [
            take(incoming_ref[pl.ds(step * members, members), :], index) for step in range(steps)
        ]
        total = pulled[0] * weight_ref[0, :, lanes]
        for step in range(1, steps):
            total = total + pulled[step] * weight_ref[step, :, lanes]
        part_ref[row, :] = own_part_ref[row, :] + jnp.sum(total, axis=0, keepdims=True)
        return carry

    lax.fori_loop(0, blocks, one_block, 0, unroll=32)

    rows = inlet_rows_ref[...]
    slope_new, slope_old, _, _ = slopes_of(rows[steps:steps + 1])
    index = jnp.broadcast_to(rows[steps + 1:steps + 2], shape).astype(jnp.int32)
    pulled = [
        take(incoming_ref[pl.ds(step * members, members), :], index) for step in range(steps)
    ]
    total = jnp.zeros(shape, F32)
    for step in range(steps):
        value = inlet_values_ref[pl.ds(step * members, members), :]
        for lag in range(steps - step):
            value = value + rows[lag:lag + 1] * pulled[step + lag]
        total = total + value * (
            slope_new * arriving_ref[pl.ds((step + 1) * members, members), :]
            + slope_old * arriving_ref[pl.ds(step * members, members), :]
        )
    at_inlet = jnp.sum(total, axis=0, keepdims=True)
    inlet = inlet_ref[...]
    inlet_block = inlet // LANES
    inlet_lane = inlet - inlet_block * LANES
    block_rows = lax.broadcasted_iota(jnp.int32, (blocks, LANES), 0)
    spread = jnp.where(block_rows == inlet_block, at_inlet, 0.0)
    lane_table = (
        lax.broadcasted_iota(jnp.int32, (LANES, LANES), 0)
        == jnp.broadcast_to(inlet_lane, (LANES, LANES))
    ).astype(F32)
    placed = lax.dot_general(
        spread, lane_table, (((1,), (1,)), ((), ())),
        precision=lax.Precision.HIGHEST, preferred_element_type=F32,
    )
    part_ref[...] = factor_ref[...] * (part_ref[...] + placed)
    mine = lax.axis_index("mem")
    piece = blocks // ranks
    for offset in range(ranks):
        target = mine ^ offset if is_power(ranks) else (mine + offset) % ranks
        pieces[offset][...] = part_ref[pl.ds(pl.multiple_of(target * piece, piece), piece), :]


def grad_kernel(
    steps, members, blocks, chunks,
    incoming_ref, own_ref, response_ref, slot_ref, rough_ref, factor_ref,
    grad_hbm, grad_ref, side_ref, sem,
):
    side_ref[...] = 1.0 / (rough_ref[...] * factor_ref[...] * (1.0 - skew_weight) + 0.5)
    shape = (members, LANES)
    part = blocks // chunks

    def one_block(block, carry):
        lanes = pl.ds(pl.multiple_of(block * LANES, LANES), LANES)
        row = pl.ds(block, 1)
        index = jnp.broadcast_to(slot_ref[row, :], shape)
        pulled = [
            take(incoming_ref[pl.ds(step * members, members), :], index) for step in range(steps)
        ]
        for step in range(steps):
            value = own_ref[step, :, lanes]
            for lag in range(steps - step):
                value = value + response_ref[lag, row, :] * pulled[step + lag]
            grad_ref[step, :, lanes] = (side_ref[row, :] * value).astype(jnp.bfloat16)
        return carry

    copies = []
    for chunk in range(chunks):
        lax.fori_loop(chunk * part, (chunk + 1) * part, one_block, 0, unroll=8)
        lanes = pl.ds(chunk * part * LANES, part * LANES)
        copies.append(pltpu.make_async_copy(
            grad_ref.at[:, :, lanes], grad_hbm.at[:, :, lanes], sem.at[chunk]
        ))
        copies[-1].start()
    for copy in copies:
        copy.wait()


def call(kernel, out_shape, scratch=(), flops=0, size=0, **specs):
    return pl.pallas_call(
        kernel,
        out_shape=out_shape,
        **specs,
        scratch_shapes=scratch,
        compiler_params=pltpu.CompilerParams(vmem_limit_bytes=VMEM_BYTES),
        cost_estimate=pl.CostEstimate(flops=flops, bytes_accessed=size, transcendentals=0),
    )


def gradients(
    stored_reach_flows, lateral, cotangent, roughness, travel_factor,
    inverse_block_matrix, down_in_block, exit_slot, inlet_reach,
):
    steps, members, reaches = cotangent.shape
    blocks = reaches // LANES
    count = lax.axis_size("net")
    ranks = lax.axis_size("mem")
    rough = roughness.reshape(blocks, LANES)
    factor = travel_factor.reshape(blocks, LANES)
    down = down_in_block.reshape(blocks, LANES)
    leave = exit_slot.reshape(blocks, LANES)
    rows = steps * members + EXTRA
    shape = jax.ShapeDtypeStruct
    work = steps * members * reaches

    hbm = pl.BlockSpec(memory_space=pltpu.HBM)

    def stay_out(array):
        return pltpu.with_memory_space_constraint(array, pltpu.HBM)

    inputs = (
        stored_reach_flows, leave, rough, factor, down, inlet_reach, inverse_block_matrix, cotangent
    )
    flows, leave, rough, factor, down, inlets, matrix, cotangent, leaving = call(
        functools.partial(fetch_kernel, steps, members, blocks, len(inputs)),
        tuple(shape(array.shape, array.dtype) for array in inputs)
        + (shape(((steps + 1) * members, LANES), F32),),
        scratch=[
            pltpu.SemaphoreType.DMA((-(-blocks // CHUNK),)),
            pltpu.SemaphoreType.DMA((len(inputs),)),
        ],
        flops=2 * LANES * work,
        size=9 * work,
        in_specs=[hbm] * len(inputs),
    )(*(stay_out(array) for array in inputs))
    own, message, response, slot, inlet_values, inlet_rows, lateral = call(
        functools.partial(local_kernel, steps, members, blocks),
        (
            shape((steps, members, reaches), F32),
            shape((rows, LANES), F32),
            shape((steps, blocks, LANES), F32),
            shape((blocks, LANES), jnp.int32),
            shape((steps * members, LANES), F32),
            shape((EXTRA, LANES), F32),
            shape(lateral.shape, lateral.dtype),
        ),
        scratch=[pltpu.VMEM((blocks, LANES), F32)] * 2 + [pltpu.SemaphoreType.DMA],
        flops=8 * LANES * work,
        size=6 * work,
        in_specs=[pl.BlockSpec()] * 7 + [hbm],
    )(cotangent, matrix, rough, factor, down, leave, inlets, stay_out(lateral))

    weight, own_part = call(
        functools.partial(weight_kernel, steps, members, blocks),
        (shape((steps, members, reaches), F32), shape((blocks, LANES), F32)),
        scratch=[pltpu.VMEM((4, blocks, LANES), F32)],
        flops=2 * LANES * work,
        size=8 * work,
    )(flows, lateral, own, response, rough, factor, down)

    stride = 1
    inner = ()
    radices = radices_of(count)
    for turn, radix in enumerate(radices[:-1]):
        received = [message]
        for offset in range(1, radix):
            received.append(exchange(message, "net", stride, radix, offset))
        if turn == 0:
            arriving = lax.ppermute(leaving, "net", [(i, i + 1) for i in range(count - 1)])
        later, message = call(
            functools.partial(group_kernel, steps, members, "net", stride, radix, len(inner)),
            (shape((rows, LANES), F32),) * 2,
            flops=20 * radix * rows * LANES,
            size=4 * radix * rows * LANES,
        )(*received, *inner)
        inner = (later,)
        stride *= radix
    radix = radices[-1]
    if len(radices) == 1:
        arriving = lax.ppermute(leaving, "net", [(i, i + 1) for i in range(count - 1)])
    received = [message] + [
        exchange(message, "net", stride, radix, offset) for offset in range(1, radix)
    ]

    piece = shape((blocks // ranks, LANES), F32)
    incoming, *pieces = call(
        functools.partial(
            sums_kernel, steps, members, blocks, ranks, stride, radix, len(inner)
        ),
        (shape((steps * members, LANES), F32),) + (piece,) * ranks,
        scratch=[pltpu.VMEM((blocks, LANES), F32)],
        flops=20 * work,
        size=4 * work,
    )(
        *received, *inner, slot, weight, own_part, factor,
        inlet_values, inlet_rows, arriving, inlets,
    )
    chunks = next(n for n in (4, 2, 1) if blocks % n == 0)
    grad_lateral = call(
        functools.partial(grad_kernel, steps, members, blocks, chunks),
        shape((steps, members, reaches), jnp.bfloat16),
        scratch=[
            pltpu.VMEM((steps, members, reaches), jnp.bfloat16),
            pltpu.VMEM((blocks, LANES), F32),
            pltpu.SemaphoreType.DMA((chunks,)),
        ],
        flops=30 * work,
        size=6 * work,
        out_specs=pl.BlockSpec(memory_space=pl.ANY),
    )(incoming, own, response, slot, rough, factor)
    total = pieces[0]
    for offset in range(1, ranks):
        back = offset if is_power(ranks) else ranks - offset
        arrived = exchange(pieces[offset], "mem", 1, ranks, back)
        total = total + arrived
    return grad_lateral, total.reshape(-1)


def solution(mesh):
    in_specs = (
        P(None, "mem", "net"),
        P(None, "mem", "net"),
        P(None, "mem", "net"),
        P("net"),
        P("net"),
        P("net", None, None),
        P("net"),
        P("net"),
        P("net", None),
    )
    out_specs = (P(None, "mem", "net"), P(("net", "mem")))
    return jax.shard_map(gradients, mesh=mesh, in_specs=in_specs, out_specs=out_specs, check_vma=False)
```

```python
import functools

import jax
import jax.numpy as jnp
from jax import lax
from jax.experimental import pallas as pl
from jax.experimental.pallas import tpu as pltpu
from jax.sharding import PartitionSpec as P


skew_weight = 0.2
LANES = 128
EXTRA = 8
F32 = jnp.float32


ROW_GATHER = lax.GatherDimensionNumbers(
    offset_dims=(), collapsed_slice_dims=(1,), start_index_map=(1,),
    operand_batching_dims=(0,), start_indices_batching_dims=(0,),
)
VMEM_BYTES = 20 << 20
GROUP = 16
CHUNK = 32


def take(values, index):
    return lax.gather(
        values, index[..., None], ROW_GATHER, (1, 1),
        mode=lax.GatherScatterMode.PROMISE_IN_BOUNDS,
    )


def weights_of(travel):
    divisor = travel * (1.0 - skew_weight) + 0.5
    weight_new = (0.5 - travel * skew_weight) / divisor
    weight_old = (0.5 + travel * skew_weight) / divisor
    weight_stay = (travel * (1.0 - skew_weight) - 0.5) / divisor
    return weight_new, weight_old, weight_stay


def slopes_of(travel):
    divisor = travel * (1.0 - skew_weight) + 0.5
    square = divisor * divisor
    return (
        -0.5 / square,
        (skew_weight - 0.5) / square,
        (1.0 - skew_weight) / square,
        (skew_weight - 1.0) / square,
    )


def levels_of(lanes):
    count = 0
    while (1 << count) < lanes:
        count += 1
    return count


def split(value):
    high = value.astype(jnp.bfloat16)
    return high, (value - high.astype(F32)).astype(jnp.bfloat16)


def multiply_series(steps, left, right):
    result = []
    for lag in range(steps):
        total = left[0] * right[lag]
        for first in range(1, lag + 1):
            total = total + left[first] * right[lag - first]
        result.append(total)
    return result


def local_kernel(
    steps, members, blocks,
    cot_ref, matrix_ref, rough_ref, factor_ref, down_ref, exit_ref, inlet_ref, lateral_hbm,
    own_ref, message_ref, response_ref, slot_ref, inlet_values_ref, inlet_rows_ref, lateral_ref,
    stay_ref, ratio_ref, lateral_sem,
):
    lateral_copy = pltpu.make_async_copy(lateral_hbm, lateral_ref, lateral_sem)
    lateral_copy.start()

    travel = rough_ref[...] * factor_ref[...]
    weight_new, weight_old, weight_stay = weights_of(travel)
    down = down_ref[...]
    lane = lax.broadcasted_iota(jnp.int32, down.shape, 1)
    interior = down < LANES
    pointer = jnp.where(interior, down, lane)
    next_new = take(weight_new, pointer)
    next_old = take(weight_old, pointer)
    ratio = jnp.where(interior, next_old / next_new, 0.0)
    stay_ref[...] = weight_stay
    ratio_ref[...] = ratio

    inlet = inlet_ref[...]
    inlet_block = inlet // LANES
    inlet_lane = inlet - inlet_block * LANES
    member_lane = jnp.broadcast_to(inlet_lane, (members, LANES))
    member_block = jnp.broadcast_to(inlet_block, (members, LANES))
    at_inlet = [jnp.zeros((members, LANES), F32)] * steps

    def solve_group(first, at_inlet):
        places = range(first, min(first + GROUP, blocks))
        tables = {
            block: jnp.concatenate(split(matrix_ref[block]), axis=1) for block in places
        }
        right, value = {}, {}
        for step in reversed(range(steps)):
            for block in places:
                lanes = pl.ds(block * LANES, LANES)
                row = pl.ds(block, 1)
                source = cot_ref[step, :, lanes]
                if step == steps - 1:
                    right[block] = source.astype(F32)
                    product = jnp.dot(source, tables[block], preferred_element_type=F32)
                    value[block] = product[:, :LANES] + product[:, LANES:]
                else:
                    right[block] = (
                        source.astype(F32)
                        + stay_ref[row, :] * value[block]
                        + ratio_ref[row, :] * (value[block] - right[block])
                    )
                    product = jnp.dot(
                        jnp.concatenate(split(right[block]), axis=0), tables[block],
                        preferred_element_type=F32,
                    )
                    value[block] = product[:members, :LANES] + (
                        product[members:, :LANES] + product[:members, LANES:]
                    )
                own_ref[step, :, lanes] = value[block]
                at_inlet[step] = jnp.where(
                    member_block == block, take(value[block], member_lane), at_inlet[step]
                )
        return at_inlet

    unit = jnp.where(exit_ref[...] >= 0, 1.0, 0.0).astype(F32)
    response = [unit]
    gain = [jnp.where(interior, next_new, 0.0)]
    base = jnp.where(interior, next_new * weight_stay + next_old, 0.0)
    for _ in range(1, steps):
        response.append(response[-1] * weight_stay)
        gain.append(base)
        base = base * weight_stay
    for level in range(levels_of(LANES)):
        pulled = [take(value, pointer) for value in response]
        added = multiply_series(steps, gain, pulled)
        response = [value + more for value, more in zip(response, added)]
        if level + 1 < levels_of(LANES):
            gain = multiply_series(steps, gain, [take(value, pointer) for value in gain])
        pointer = take(pointer, pointer)
    slot = take(exit_ref[...], pointer)
    slot = jnp.maximum(slot, 0)
    slot_ref[...] = slot
    for lag in range(steps):
        response_ref[lag] = response[lag]

    lane_rows = jnp.broadcast_to(inlet_lane, (blocks, LANES))
    block_rows = lax.broadcasted_iota(jnp.int32, (blocks, LANES), 0)
    chosen = block_rows == jnp.broadcast_to(inlet_block, (blocks, LANES))

    def at_inlets(rows):
        return jnp.sum(jnp.where(chosen, take(rows, lane_rows), 0.0), axis=0, keepdims=True)

    travel_in = at_inlets(travel)
    slot_in = at_inlets(slot.astype(F32))
    response_in = [at_inlets(value) for value in response]
    new_in, old_in, _ = weights_of(travel_in)

    for first in range(0, blocks, GROUP):
        at_inlet = solve_group(first, list(at_inlet))

    for step in range(steps):
        rows = pl.ds(step * members, members)
        inlet_values_ref[rows, :] = at_inlet[step]
        outgoing = new_in * at_inlet[step]
        if step + 1 < steps:
            outgoing = outgoing + old_in * at_inlet[step + 1]
        message_ref[rows, :] = outgoing
    tail = []
    for lag in range(steps):
        coefficient = new_in * response_in[lag]
        if lag > 0:
            coefficient = coefficient + old_in * response_in[lag - 1]
        tail.append(coefficient)
    message_ref[pl.ds(steps * members, EXTRA), :] = eight_rows(tail + [slot_in])
    inlet_rows_ref[...] = eight_rows(response_in + [travel_in, slot_in])
    lateral_copy.wait()


def fetch_kernel(steps, members, blocks, count, *refs):
    sources, targets = refs[:count], refs[count:2 * count]
    leaving_ref, flow_sem, sem = refs[2 * count:]
    flow_hbm, flow_ref = sources[0], targets[0]
    exit_ref = targets[1]
    flow_copies = []
    for turn, first in enumerate(range(0, blocks, CHUNK)):
        lanes = pl.ds(first * LANES, min(CHUNK, blocks - first) * LANES)
        flow_copies.append(pltpu.make_async_copy(
            flow_hbm.at[:, :, lanes], flow_ref.at[:, :, lanes], flow_sem.at[turn]
        ))
    copies = [
        pltpu.make_async_copy(sources[i], targets[i], sem.at[i]) for i in range(1, count)
    ]
    copies[0].start()
    for copy in flow_copies:
        copy.start()
    for copy in copies[1:]:
        copy.start()
    copies[0].wait()
    sub = lax.broadcasted_iota(jnp.int32, (LANES, LANES), 0)
    total = None
    for block in range(blocks):
        if block % CHUNK == 0:
            flow_copies[block // CHUNK].wait()
        lanes = pl.ds(block * LANES, LANES)
        table = (sub == exit_ref[pl.ds(block, 1), :]).astype(F32).astype(jnp.bfloat16)
        flows = flow_ref[:, :, lanes].reshape((steps + 1) * members, LANES)
        part = lax.dot_general(
            flows, table, (((1,), (1,)), ((), ())), preferred_element_type=F32
        )
        total = part if total is None else total + part
    leaving_ref[...] = total
    for copy in copies[1:]:
        copy.wait()


def eight_rows(rows):
    rows = list(rows)
    while len(rows) % EXTRA:
        rows.append(jnp.zeros_like(rows[0]))
    return jnp.concatenate(rows, axis=0)


def compose(steps, members, upper, lower):
    values, coefficients, slot = upper
    below, below_coefficients, below_slot = lower
    index = jnp.broadcast_to(slot, (members, LANES)).astype(jnp.int32)
    pulled = [take(value, index) for value in below]
    result = []
    for step in range(steps):
        total = values[step]
        for lag in range(steps - step):
            total = total + coefficients[lag] * pulled[step + lag]
        result.append(total)
    if below_coefficients is None:
        return result, None, None
    table = eight_rows(list(below_coefficients) + [below_slot])
    table = take(table, jnp.broadcast_to(slot, table.shape).astype(jnp.int32))
    combined = multiply_series(
        steps, coefficients, [table[lag:lag + 1] for lag in range(steps)]
    )
    return result, combined, table[steps:steps + 1]


def read_message(steps, members, ref):
    values = [ref[pl.ds(step * members, members), :] for step in range(steps)]
    tail = ref[pl.ds(steps * members, EXTRA), :]
    return values, [tail[lag:lag + 1] for lag in range(steps)], tail[steps:steps + 1]


def write_message(steps, members, ref, message):
    values, coefficients, slot = message
    for step in range(steps):
        ref[pl.ds(step * members, members), :] = values[step]
    ref[pl.ds(steps * members, EXTRA), :] = eight_rows(list(coefficients) + [slot])


def identity_message(steps, members):
    zero = jnp.zeros((members, LANES), F32)
    row = jnp.zeros((1, LANES), F32)
    lane = lax.broadcasted_iota(jnp.int32, (8, LANES), 1).astype(F32)[0:1]
    return [zero] * steps, [row + 1.0] + [row] * (steps - 1), lane


def digit_of(axis, stride, radix):
    return (lax.axis_index(axis) // stride) % radix


def group_kernel(steps, members, axis, stride, radix, has_inner, values_only, *refs):
    messages = refs[:radix]
    inner = refs[radix] if has_inner else None
    outs = refs[radix + has_inner:]
    digit = digit_of(axis, stride, radix)
    for mine in range(radix):
        @pl.when(digit == mine)
        def _(mine=mine):
            total = None
            later = None
            for other in reversed(range(radix)):
                message = read_message(steps, members, messages[source_of(mine, other, radix)])
                total = message if total is None else compose(steps, members, message, total)
                if other == mine + 1:
                    later = total
            if later is None:
                later = identity_message(steps, members)
            if has_inner:
                later = compose(steps, members, read_message(steps, members, inner), later)
            write_message(steps, members, outs[0], later)
            if values_only:
                for step in range(steps):
                    outs[1][pl.ds(step * members, members), :] = total[0][step]
            else:
                write_message(steps, members, outs[1], total)


def last_round(steps, members, axis, stride, radix, messages, inner, out):
    digit = digit_of(axis, stride, radix)
    for mine in range(radix):
        @pl.when(digit == mine)
        def _(mine=mine):
            value = [jnp.zeros((members, LANES), F32)] * steps
            for other in reversed(range(mine + 1, radix)):
                source = messages[source_of(mine, other, radix)]
                if other == radix - 1:
                    value = [source[pl.ds(step * members, members), :] for step in range(steps)]
                else:
                    message = read_message(steps, members, source)
                    value = compose(steps, members, message, (value, None, None))[0]
            if inner is not None:
                within = read_message(steps, members, inner)
                if mine == radix - 1:
                    value = within[0]
                else:
                    value = compose(steps, members, within, (value, None, None))[0]
            for step in range(steps):
                out[pl.ds(step * members, members), :] = value[step]


def is_power(number):
    return number & (number - 1) == 0


def source_of(mine, other, radix):
    return mine ^ other if is_power(radix) else (other - mine) % radix


def exchange(value, axis, stride, radix, offset):
    pairs = []
    for device in range(lax.axis_size(axis)):
        digit = (device // stride) % radix
        source = digit ^ offset if is_power(radix) else (digit + offset) % radix
        pairs.append((device + (source - digit) * stride, device))
    return lax.ppermute(value, axis, pairs)


def radices_of(count):
    radices = []
    while count > 1:
        radix = next(r for r in (4, 2, 3, 5, 7, count) if count % r == 0)
        radices.append(radix)
        count //= radix
    return radices or [1]


def weight_kernel(
    steps, members, blocks,
    flow_ref, lateral_ref, own_ref, response_ref, rough_ref, factor_ref, down_ref,
    weight_ref, part_ref, slopes_ref,
):
    slopes = slopes_of(rough_ref[...] * factor_ref[...])
    for i in range(4):
        slopes_ref[i] = slopes[i]
    sub = lax.broadcasted_iota(jnp.int32, (LANES, LANES), 0)

    def one_block(block, carry):
        lanes = pl.ds(pl.multiple_of(block * LANES, LANES), LANES)
        row = pl.ds(block, 1)
        table = (sub == down_ref[row, :]).astype(F32).astype(jnp.bfloat16)
        flows = flow_ref[:, :, lanes].reshape((steps + 1) * members, LANES)
        inflow = lax.dot_general(
            flows, table, (((1,), (1,)), ((), ())), preferred_element_type=F32
        )
        new, old, stay, side = (slopes_ref[i, row, :] for i in range(4))
        total = jnp.zeros((members, LANES), F32)
        weights = []
        for step in range(steps):
            now = inflow[(step + 1) * members:(step + 2) * members]
            prior = inflow[step * members:(step + 1) * members]
            weight = (
                new * now
                + old * prior
                + stay * flow_ref[step, :, lanes].astype(F32)
                + side * lateral_ref[step, :, lanes].astype(F32)
            )
            weights.append(weight)
            total = total + weight * own_ref[step, :, lanes]
            folded = response_ref[0, row, :] * weight
            for lag in range(1, step + 1):
                folded = folded + response_ref[lag, row, :] * weights[step - lag]
            weight_ref[step, :, lanes] = folded
        part_ref[row, :] = jnp.sum(total, axis=0, keepdims=True)
        return carry

    lax.fori_loop(0, blocks, one_block, 0, unroll=8)


def sums_kernel(steps, members, blocks, ranks, stride, radix, has_inner, *refs):
    messages, refs = refs[:radix], refs[radix:]
    inner, refs = (refs[0], refs[1:]) if has_inner else (None, refs)
    (
        slot_ref, weight_ref, own_part_ref, factor_ref,
        inlet_values_ref, inlet_rows_ref, arriving_ref, inlet_ref,
    ) = refs[:8]
    incoming_ref = refs[8]
    pieces = refs[9:9 + ranks]
    (part_ref,) = refs[9 + ranks:]
    last_round(steps, members, "net", stride, radix, messages, inner, incoming_ref)
    shape = (members, LANES)

    def one_block(block, carry):
        lanes = pl.ds(pl.multiple_of(block * LANES, LANES), LANES)
        row = pl.ds(block, 1)
        index = jnp.broadcast_to(slot_ref[row, :], shape)
        pulled = [
            take(incoming_ref[pl.ds(step * members, members), :], index) for step in range(steps)
        ]
        total = pulled[0] * weight_ref[0, :, lanes]
        for step in range(1, steps):
            total = total + pulled[step] * weight_ref[step, :, lanes]
        part_ref[row, :] = own_part_ref[row, :] + jnp.sum(total, axis=0, keepdims=True)
        return carry

    lax.fori_loop(0, blocks, one_block, 0, unroll=32)

    rows = inlet_rows_ref[...]
    slope_new, slope_old, _, _ = slopes_of(rows[steps:steps + 1])
    index = jnp.broadcast_to(rows[steps + 1:steps + 2], shape).astype(jnp.int32)
    pulled = [
        take(incoming_ref[pl.ds(step * members, members), :], index) for step in range(steps)
    ]
    total = jnp.zeros(shape, F32)
    for step in range(steps):
        value = inlet_values_ref[pl.ds(step * members, members), :]
        for lag in range(steps - step):
            value = value + rows[lag:lag + 1] * pulled[step + lag]
        total = total + value * (
            slope_new * arriving_ref[pl.ds((step + 1) * members, members), :]
            + slope_old * arriving_ref[pl.ds(step * members, members), :]
        )
    at_inlet = jnp.sum(total, axis=0, keepdims=True)
    inlet = inlet_ref[...]
    inlet_block = inlet // LANES
    inlet_lane = inlet - inlet_block * LANES
    block_rows = lax.broadcasted_iota(jnp.int32, (blocks, LANES), 0)
    spread = jnp.where(block_rows == inlet_block, at_inlet, 0.0)
    lane_table = (
        lax.broadcasted_iota(jnp.int32, (LANES, LANES), 0)
        == jnp.broadcast_to(inlet_lane, (LANES, LANES))
    ).astype(F32)
    placed = lax.dot_general(
        spread, lane_table, (((1,), (1,)), ((), ())),
        precision=lax.Precision.HIGHEST, preferred_element_type=F32,
    )
    part_ref[...] = factor_ref[...] * (part_ref[...] + placed)
    mine = lax.axis_index("mem")
    piece = blocks // ranks
    for offset in range(ranks):
        target = mine ^ offset if is_power(ranks) else (mine + offset) % ranks
        pieces[offset][...] = part_ref[pl.ds(pl.multiple_of(target * piece, piece), piece), :]


def grad_kernel(
    steps, members, blocks, chunks,
    incoming_ref, own_ref, response_ref, slot_ref, rough_ref, factor_ref,
    grad_hbm, grad_ref, side_ref, sem,
):
    side_ref[...] = 1.0 / (rough_ref[...] * factor_ref[...] * (1.0 - skew_weight) + 0.5)
    shape = (members, LANES)
    part = blocks // chunks

    def one_block(block, carry):
        lanes = pl.ds(pl.multiple_of(block * LANES, LANES), LANES)
        row = pl.ds(block, 1)
        index = jnp.broadcast_to(slot_ref[row, :], shape)
        pulled = [
            take(incoming_ref[pl.ds(step * members, members), :], index) for step in range(steps)
        ]
        for step in range(steps):
            value = own_ref[step, :, lanes]
            for lag in range(steps - step):
                value = value + response_ref[lag, row, :] * pulled[step + lag]
            grad_ref[step, :, lanes] = (side_ref[row, :] * value).astype(jnp.bfloat16)
        return carry

    copies = []
    for chunk in range(chunks):
        lax.fori_loop(chunk * part, (chunk + 1) * part, one_block, 0, unroll=8)
        lanes = pl.ds(chunk * part * LANES, part * LANES)
        copies.append(pltpu.make_async_copy(
            grad_ref.at[:, :, lanes], grad_hbm.at[:, :, lanes], sem.at[chunk]
        ))
        copies[-1].start()
    for copy in copies:
        copy.wait()


def call(kernel, out_shape, scratch=(), flops=0, size=0, **specs):
    return pl.pallas_call(
        kernel,
        out_shape=out_shape,
        **specs,
        scratch_shapes=scratch,
        compiler_params=pltpu.CompilerParams(vmem_limit_bytes=VMEM_BYTES),
        cost_estimate=pl.CostEstimate(flops=flops, bytes_accessed=size, transcendentals=0),
    )


def gradients(
    stored_reach_flows, lateral, cotangent, roughness, travel_factor,
    inverse_block_matrix, down_in_block, exit_slot, inlet_reach,
):
    steps, members, reaches = cotangent.shape
    blocks = reaches // LANES
    count = lax.axis_size("net")
    ranks = lax.axis_size("mem")
    rough = roughness.reshape(blocks, LANES)
    factor = travel_factor.reshape(blocks, LANES)
    down = down_in_block.reshape(blocks, LANES)
    leave = exit_slot.reshape(blocks, LANES)
    rows = steps * members + EXTRA
    shape = jax.ShapeDtypeStruct
    work = steps * members * reaches

    hbm = pl.BlockSpec(memory_space=pltpu.HBM)

    def stay_out(array):
        return pltpu.with_memory_space_constraint(array, pltpu.HBM)

    inputs = (
        stored_reach_flows, leave, rough, factor, down, inlet_reach, inverse_block_matrix, cotangent
    )
    flows, leave, rough, factor, down, inlets, matrix, cotangent, leaving = call(
        functools.partial(fetch_kernel, steps, members, blocks, len(inputs)),
        tuple(shape(array.shape, array.dtype) for array in inputs)
        + (shape(((steps + 1) * members, LANES), F32),),
        scratch=[
            pltpu.SemaphoreType.DMA((-(-blocks // CHUNK),)),
            pltpu.SemaphoreType.DMA((len(inputs),)),
        ],
        flops=2 * LANES * work,
        size=9 * work,
        in_specs=[hbm] * len(inputs),
    )(*(stay_out(array) for array in inputs))
    own, message, response, slot, inlet_values, inlet_rows, lateral = call(
        functools.partial(local_kernel, steps, members, blocks),
        (
            shape((steps, members, reaches), F32),
            shape((rows, LANES), F32),
            shape((steps, blocks, LANES), F32),
            shape((blocks, LANES), jnp.int32),
            shape((steps * members, LANES), F32),
            shape((EXTRA, LANES), F32),
            shape(lateral.shape, lateral.dtype),
        ),
        scratch=[pltpu.VMEM((blocks, LANES), F32)] * 2 + [pltpu.SemaphoreType.DMA],
        flops=8 * LANES * work,
        size=6 * work,
        in_specs=[pl.BlockSpec()] * 7 + [hbm],
    )(cotangent, matrix, rough, factor, down, leave, inlets, stay_out(lateral))

    weight, own_part = call(
        functools.partial(weight_kernel, steps, members, blocks),
        (shape((steps, members, reaches), F32), shape((blocks, LANES), F32)),
        scratch=[pltpu.VMEM((4, blocks, LANES), F32)],
        flops=2 * LANES * work,
        size=8 * work,
    )(flows, lateral, own, response, rough, factor, down)

    stride = 1
    inner = ()
    radices = radices_of(count)
    for turn, radix in enumerate(radices[:-1]):
        received = [message]
        for offset in range(1, radix):
            received.append(exchange(message, "net", stride, radix, offset))
        if turn == 0:
            arriving = lax.ppermute(leaving, "net", [(i, i + 1) for i in range(count - 1)])
        values_only = turn == len(radices) - 2 and radices[-1] == 2
        later, message = call(
            functools.partial(
                group_kernel, steps, members, "net", stride, radix, len(inner), values_only
            ),
            (
                shape((rows, LANES), F32),
                shape((steps * members if values_only else rows, LANES), F32),
            ),
            flops=20 * radix * rows * LANES,
            size=4 * radix * rows * LANES,
        )(*received, *inner)
        inner = (later,)
        stride *= radix
    radix = radices[-1]
    if len(radices) == 1:
        arriving = lax.ppermute(leaving, "net", [(i, i + 1) for i in range(count - 1)])
    received = [message] + [
        exchange(message, "net", stride, radix, offset) for offset in range(1, radix)
    ]

    piece = shape((blocks // ranks, LANES), F32)
    incoming, *pieces = call(
        functools.partial(
            sums_kernel, steps, members, blocks, ranks, stride, radix, len(inner)
        ),
        (shape((steps * members, LANES), F32),) + (piece,) * ranks,
        scratch=[pltpu.VMEM((blocks, LANES), F32)],
        flops=20 * work,
        size=4 * work,
    )(
        *received, *inner, slot, weight, own_part, factor,
        inlet_values, inlet_rows, arriving, inlets,
    )
    chunks = next(n for n in (4, 2, 1) if blocks % n == 0)
    grad_lateral = call(
        functools.partial(grad_kernel, steps, members, blocks, chunks),
        shape((steps, members, reaches), jnp.bfloat16),
        scratch=[
            pltpu.VMEM((steps, members, reaches), jnp.bfloat16),
            pltpu.VMEM((blocks, LANES), F32),
            pltpu.SemaphoreType.DMA((chunks,)),
        ],
        flops=30 * work,
        size=6 * work,
        out_specs=pl.BlockSpec(memory_space=pl.ANY),
    )(incoming, own, response, slot, rough, factor)
    total = pieces[0]
    for offset in range(1, ranks):
        back = offset if is_power(ranks) else ranks - offset
        arrived = exchange(pieces[offset], "mem", 1, ranks, back)
        total = total + arrived
    return grad_lateral, total.reshape(-1)


def solution(mesh):
    in_specs = (
        P(None, "mem", "net"),
        P(None, "mem", "net"),
        P(None, "mem", "net"),
        P("net"),
        P("net"),
        P("net", None, None),
        P("net"),
        P("net"),
        P("net", None),
    )
    out_specs = (P(None, "mem", "net"), P(("net", "mem")))
    return jax.shard_map(gradients, mesh=mesh, in_specs=in_specs, out_specs=out_specs, check_vma=False)
```
